32 devices in a mesh: tier: 16 (over z, x, core), sys: 2 (over y).
Axes of the slice: x: 2, y: 2, z: 4, core: 2. Of those that a mesh axis runs over, the one named last changes fastest.
Arguments:
- state: float32 [64, 2, 512, 512], P('tier', None, 'sys'), may hold values from -6 to 6
- slope: float32 [64, 2, 512, 512], P('tier', None, 'sys'), may hold values from -6 to 6
- counts: int32 [16], replicated, may hold values from 1 to 4, 32 in all
- links: int32 [4, 64, 24], P(None, 'tier'), may hold values from 0 to 63, as said below
- mode_site: int32 [12], replicated, may hold values from 0 to 511, as said below
- mode_coef: float32 [2, 12], replicated, may hold values from -3 to 3
- mode_rate: float32 [12], replicated, may hold values from 0.01 to 0.1
- h_bands: float32 [9, 512], replicated, may hold values from -3 to 3
Outputs:
- slope_next: float32 [64, 2, 512, 512], P('tier', None, 'sys')
- partial_sum: float32 [64, 2, 512, 512], P('tier', None, 'sys')
The draws below stay inside these ranges and needn't reach their ends.
Inputs may be any that keep to these rules, and one draw needn't show every extreme that they name: Index d of tier holds counts[d] live auxiliary operators, in its first slots; the counts sum to 32. links[0] is a global slot (index of tier times 4 plus the slot), links[1] a mode below 12, links[2] is 0 or 1, links[3] is 1 or 2. Each slot has exactly one link with direction 0 and one with direction 1 for every mode. Of the 96 links of the slots of one index of tier, exactly 6 name slots of each index of tier; of the links whose mode k has k // 6 equal to one row block's number, at most 4 name slots of one index of tier, and in every row block some index of tier is named by exactly 4 of them. `mode_site`: mode k's site lies in row block k // 6, that is in rows (k // 6) * 256 to (k // 6) * 256 + 255; the sites are distinct.
All inputs are finite; a program needn't handle non-finite values.
Results may differ from the reference program's by a relative error of at most 0.0003.
Values sent between devices are 32-bit elements; how exact they have to be, the bound alone decides.
A program may use at most 64 MiB of HBM per device.

```python
import math
import jax
import jax.numpy as jnp
import numpy as np
from jax import lax

LEVELS = 512
BAND = 8
MODES_BLK = 6
SLOTS = 4
SLOTS_ALL = 64
ADOS = 32
MODES = 12
LINKS = 24
ROWS_DEV = 256
N_TIER = 16
N_SYS = 2


def draw_links(key, part):
    per_block = SLOTS * 2 * MODES_BLK

    def one_device(device_key):
        key_holder, key_order, key_slot, key_level = jax.random.split(device_key, 4)
        holders = jax.random.permutation(key_holder, N_TIER).astype(jnp.int32)
        order = jax.vmap(lambda block_key: jax.random.permutation(block_key, per_block))(jax.random.split(key_order, N_SYS)).astype(jnp.int32)
        base = jnp.arange(N_SYS, dtype=jnp.int32)[:, None] * per_block + order
        holder = holders[base // 2 % N_TIER]
        within = jnp.arange(per_block, dtype=jnp.int32)
        target_slot = jax.random.randint(key_slot, (N_SYS, per_block), 0, SLOTS, dtype=jnp.int32)
        mode_pick = jnp.arange(N_SYS, dtype=jnp.int32)[:, None] * MODES_BLK + (within // 2 % MODES_BLK)[None, :]
        link_kind = jnp.broadcast_to((within % 2)[None, :], (N_SYS, per_block))
        link_level = jax.random.randint(key_level, (N_SYS, per_block), 1, 3, dtype=jnp.int32)
        stacked = jnp.stack([holder * SLOTS + target_slot, mode_pick, link_kind, link_level])
        stacked = stacked.reshape(4, N_SYS, SLOTS, 2 * MODES_BLK)
        return jnp.transpose(stacked, (0, 2, 1, 3)).reshape(4, SLOTS, LINKS)
    devices = jax.vmap(one_device)(jax.random.split(jax.random.fold_in(key, 11), N_TIER))
    return jnp.transpose(devices, (1, 0, 2, 3)).reshape(4, SLOTS_ALL, LINKS).astype(jnp.int32)


def draw_mode_site(key, part):

    def one_block(block_key):
        return jax.random.permutation(block_key, ROWS_DEV)[:MODES_BLK].astype(jnp.int32)
    chosen = jax.vmap(one_block)(jax.random.split(jax.random.fold_in(key, 23), N_SYS))
    offsets = ROWS_DEV * jnp.arange(N_SYS, dtype=jnp.int32)[:, None]
    return (chosen + offsets).reshape(MODES).astype(jnp.int32)


def level_of(own_key, shape, shards, least, top_value):
    def one(axis_at, parts):
        steps = jax.random.uniform(jax.random.fold_in(jax.random.fold_in(own_key, 6), axis_at), (parts,), jnp.float32, least / len(shards), top_value / len(shards))
        return jnp.repeat(jnp.exp(steps), shape[axis_at] // parts).reshape((-1,) + (1,) * (len(shape) - axis_at - 1))

    level = one(*shards[0])
    for cut in shards[1:]:
        level = level * one(*cut)
    return level


def length_profile(count, total, bound, lean):
    loads = [(1 << 20) // math.isqrt(grade ** lean) + 1 for grade in range(2, count + 1)]
    spare, given = total - bound - (count - 1), [1] * (count - 1)
    while spare > 0:
        movable = [i for i in range(count - 1) if given[i] < bound]
        whole, remaining = sum([loads[i] for i in movable]), spare
        for i in movable:
            more = min(bound - given[i], max(1, remaining * loads[i] // whole), spare)
            given[i] = given[i] + more
            spare = spare - more
    return np.array([bound] + given)


def ragged_sizes(stream_key, count, total, reach, lean):
    if count == 2:
        one = jax.random.randint(stream_key, (), max(1, total - reach), min(reach, total - 1) + 1)
        return jnp.stack([one, total - one])
    lengths = jnp.asarray(length_profile(count, total, reach, lean), jnp.int32)
    twos = (count - 1) // 2
    source_of, sink = lengths[1:1 + 2 * twos:2], lengths[2:2 + 2 * twos:2]
    slack = jnp.minimum(source_of - 1, reach - sink)
    shifted = jax.random.randint(jax.random.fold_in(stream_key, 1), (twos,), 0, 1 << 20) % (slack + 1)
    lengths = lengths.at[1:1 + 2 * twos:2].set(source_of - shifted).at[2:2 + 2 * twos:2].set(sink + shifted)
    return lengths[jax.random.permutation(jax.random.fold_in(stream_key, 2), count)]


def centred(rng, extent, width, most, shards=(), kind=jnp.bfloat16):
    values = width * jax.random.normal(rng, extent, jnp.float32)
    if shards:
        values = values * level_of(rng, extent, shards, -0.22, 0.18)
    return jnp.clip(values, -most, most).astype(kind)


def setup_inputs(seed: int = 0) -> dict:
    seeds = jax.random.split(jax.random.key(seed), 9)
    state = centred(seeds[0], (SLOTS_ALL, 2, LEVELS, LEVELS), 1.0, 6.0, ((0, 16), (2, 2)), jnp.float32)
    slope = centred(seeds[1], (SLOTS_ALL, 2, LEVELS, LEVELS), 1.0, 6.0, ((0, 16), (2, 2)), jnp.float32)
    counts = ragged_sizes(seeds[2], N_TIER, ADOS, SLOTS, 2).astype(jnp.int32)
    links = draw_links(jax.random.fold_in(seeds[8], 71), 0)
    mode_site = draw_mode_site(jax.random.fold_in(seeds[8], 71), 0)
    mode_coef = centred(seeds[5], (2, MODES), 0.5, 3.0, (), jnp.float32)
    mode_rate = jnp.clip(jnp.exp(jax.random.uniform(seeds[6], (MODES,), jnp.float32, math.log(0.01), math.log(0.1))), 0.01, 0.1)
    h_bands = centred(seeds[7], (BAND + 1, LEVELS), 0.5, 3.0, (), jnp.float32)
    return {"state": state, "slope": slope, "counts": counts, "links": links, "mode_site": mode_site, "mode_coef": mode_coef, "mode_rate": mode_rate, "h_bands": h_bands}


step_size = 0.05


def shifted_band(h_bands):
    band_width = h_bands.shape[0] - 1
    length = h_bands.shape[1]
    padded = jnp.pad(h_bands, ((0, 0), (band_width, 0)))
    return jnp.stack([padded[offset, band_width - offset:band_width - offset + length] for offset in range(band_width + 1)])


def band_rows(padded, upper_band, lower_band, band_width):
    length = upper_band.shape[1]
    summed = upper_band[0][:, None] * padded[..., band_width:band_width + length, :]
    for offset in range(1, band_width + 1):
        summed = summed + upper_band[offset][:, None] * padded[..., band_width + offset:band_width + offset + length, :]
        summed = summed + lower_band[offset][:, None] * padded[..., band_width - offset:band_width - offset + length, :]
    return summed


def band_cols(field, upper_band, lower_band, band_width):
    length = field.shape[-1]
    padded = jnp.pad(field, ((0, 0),) * (field.ndim - 1) + ((band_width, band_width),))
    summed = upper_band[0] * field
    for offset in range(1, band_width + 1):
        summed = summed + upper_band[offset] * padded[..., band_width + offset:band_width + offset + length]
        summed = summed + lower_band[offset] * padded[..., band_width - offset:band_width - offset + length]
    return summed


def reference(state, slope, counts, links, mode_site, mode_coef, mode_rate, h_bands):
    midpoint = state + (0.5 * step_size) * slope
    every_slot = jnp.arange(SLOTS_ALL, dtype=jnp.int32)
    live = (every_slot % SLOTS < counts[every_slot // SLOTS]).astype(jnp.float32)
    lower_band = shifted_band(h_bands)

    def derive(carry, inputs):
        field, link_set = inputs
        neighbour = link_set[0]
        link_mode = link_set[1]
        link_kind = link_set[2]
        link_level = link_set[3].astype(jnp.float32)
        sites = mode_site[link_mode]
        downward = link_kind == 1
        neighbour_live = live[neighbour]
        weight_re = jnp.where(downward, link_level * mode_coef[0][link_mode], 1.0) * neighbour_live
        weight_im = jnp.where(downward, link_level * mode_coef[1][link_mode], 0.0) * neighbour_live
        damping = jnp.sum(jnp.where(downward, link_level * mode_rate[link_mode], 0.0))
        column_part = midpoint[neighbour, :, :, sites]
        row_part = midpoint[neighbour, :, sites, :]
        padded = jnp.pad(field, ((0, 0), (BAND, BAND), (0, 0)))
        commuted = band_rows(padded, h_bands, lower_band, BAND) - band_cols(field, h_bands, lower_band, BAND)
        deriv_re = commuted[1] - damping * field[0]
        deriv_im = -commuted[0] - damping * field[1]
        col_re = -(weight_re[:, None] * column_part[:, 1] - weight_im[:, None] * column_part[:, 0])
        col_im = weight_re[:, None] * column_part[:, 0] + weight_im[:, None] * column_part[:, 1]
        row_re = weight_re[:, None] * row_part[:, 1] + weight_im[:, None] * row_part[:, 0]
        row_im = -(weight_re[:, None] * row_part[:, 0] - weight_im[:, None] * row_part[:, 1])
        deriv_re = deriv_re.at[:, sites].add(col_re.T)
        deriv_im = deriv_im.at[:, sites].add(col_im.T)
        deriv_re = deriv_re.at[sites, :].add(row_re)
        deriv_im = deriv_im.at[sites, :].add(row_im)
        return carry, jnp.stack([deriv_re, deriv_im])

    _, derived = lax.scan(derive, jnp.zeros((), jnp.float32), (midpoint, jnp.moveaxis(links, 1, 0)))
    slope_next = derived * live[:, None, None, None]
    partial_sum = (state + (step_size / 6.0) * slope + (step_size / 3.0) * slope_next) * live[:, None, None, None]
    return slope_next, partial_sum
```

```python
import functools

import jax
import jax.numpy as jnp
from jax import lax
from jax.experimental import pallas as pl
from jax.experimental.pallas import tpu as pltpu
from jax.sharding import PartitionSpec as P

step_size = 0.05
MESH = pl.DeviceIdType.MESH
f32 = jnp.float32
bf16 = jnp.bfloat16


def up(value, unit):
    return (value + unit - 1) // unit * unit


def split(value):
    hi = value.astype(bf16)
    lo = (value - hi.astype(f32)).astype(bf16)
    return hi, lo


def mm(a, b):
    return lax.dot_general(a, b, (((1,), (0,)), ((), ())), preferred_element_type=f32)


def mm_nt(a, b):
    return lax.dot_general(a, b, (((1,), (1,)), ((), ())), preferred_element_type=f32)


def mm3(a, b):
    a_hi, a_lo = split(a)
    b_hi, b_lo = split(b)
    return mm(a_hi, b_hi) + (mm(a_hi, b_lo) + mm(a_lo, b_hi))


def exchange_kernel(
    dims,
    req_ref,
    lane_ref,
    site_ref,
    damp_ref,
    neg_h_ref,
    loc_h_ref,
    halo_h_ref,
    mix_c_ref,
    mix_r_ref,
    state_hbm,
    slope_hbm,
    d_hbm,
    c_ref,
    r_ref,
    st,
    sl,
    z_hi,
    z_lo,
    d_buf,
    req_in,
    halo_st,
    halo_sl,
    col_acc,
    row_pack,
    sel_c,
    sel_r,
    send_c,
    send_r,
    recv_c,
    recv_r,
    load_sem,
    out_sem,
    req_send,
    req_recv,
    halo_send,
    halo_recv,
    c_send,
    c_recv,
    r_send,
    r_recv,
):
    tiers, systems, slots, modes, block, edge, cw, rw = dims
    rows, levels = st.shape[1], st.shape[2]
    me = lax.axis_index("tier")
    sy = lax.axis_index("sys")
    planes = slots * 2

    def load(p):
        g, c = p // 2, p % 2
        return (
            pltpu.make_async_copy(state_hbm.at[g, c], st.at[p], load_sem.at[0, p]),
            pltpu.make_async_copy(slope_hbm.at[g, c], sl.at[p], load_sem.at[1, p]),
        )

    for p in range(planes):
        for copy in load(p):
            copy.start()

    barrier = pltpu.get_barrier_semaphore()

    def greet(i, carry):
        pl.semaphore_signal(
            barrier, inc=1, device_id=(lax.rem(me + i, tiers), sy), device_id_type=MESH
        )
        return carry

    lax.fori_loop(1, tiers, greet, 0)

    @pl.when(sy > 0)
    def _():
        pl.semaphore_signal(barrier, inc=1, device_id=(me, sy - 1), device_id_type=MESH)

    @pl.when(sy < systems - 1)
    def _():
        pl.semaphore_signal(barrier, inc=1, device_id=(me, sy + 1), device_id_type=MESH)

    inner = (sy > 0).astype(jnp.int32) + (sy < systems - 1).astype(jnp.int32)
    pl.semaphore_wait(barrier, tiers - 1 + inner)

    def send(src, dst, send_sem, recv_sem, i):
        peer = lax.rem(me + i, tiers)
        return pltpu.make_async_remote_copy(
            src_ref=src.at[peer],
            dst_ref=dst.at[me],
            send_sem=send_sem.at[i],
            recv_sem=recv_sem.at[i],
            device_id=(peer, sy),
            device_id_type=MESH,
        )

    def receive(src, dst, send_sem, recv_sem, i):
        peer = lax.rem(me + tiers - i, tiers)
        return pltpu.make_async_remote_copy(
            src_ref=src.at[peer],
            dst_ref=dst.at[peer],
            send_sem=send_sem.at[i],
            recv_sem=recv_sem.at[i],
            device_id=(peer, sy),
            device_id_type=MESH,
        )

    def req_start(i, carry):
        send(req_ref, req_in, req_send, req_recv, i).start()
        return carry

    lax.fori_loop(1, tiers, req_start, 0)

    def halo(side):
        first = rows - edge if side == 0 else 0
        target = sy + 1 if side == 0 else sy - 1
        return [
            pltpu.make_async_remote_copy(
                src_ref=src.at[:, :, pl.ds(first, edge), :],
                dst_ref=dst.at[side],
                send_sem=halo_send.at[side, n],
                recv_sem=halo_recv.at[side, n],
                device_id=(me, target),
                device_id_type=MESH,
            )
            for n, (src, dst) in enumerate(((state_hbm, halo_st), (slope_hbm, halo_sl)))
        ]

    @pl.when(sy < systems - 1)
    def _():
        for copy in halo(0):
            copy.start()

    @pl.when(sy > 0)
    def _():
        for copy in halo(1):
            copy.start()

    @pl.when(sy == 0)
    def _():
        halo_st[0] = jnp.zeros_like(halo_st[0])
        halo_sl[0] = jnp.zeros_like(halo_sl[0])

    @pl.when(sy == systems - 1)
    def _():
        halo_st[1] = jnp.zeros_like(halo_st[1])
        halo_sl[1] = jnp.zeros_like(halo_sl[1])

    req_in[me] = req_ref[me]
    row_pack[...] = jnp.zeros_like(row_pack)
    width = col_acc.shape[-1]
    lane_site = lane_ref[0:1, :]
    lane_slot = lane_ref[1:2, :]
    level_at = lax.broadcasted_iota(jnp.int32, (levels, width), 0)
    for g in range(slots):
        pick = jnp.where((level_at == lane_site) & (lane_slot == g), 1.0, 0.0).astype(bf16)
        for c in range(2):
            p = g * 2 + c
            for copy in load(p):
                copy.wait()
            hi, lo = split(st[p] + (0.5 * step_size) * sl[p])
            z_hi[p] = hi
            z_lo[p] = lo
            col_hi = mm(hi, pick)
            col_lo = mm(lo, pick)
            if g == 0:
                col_acc[c] = col_hi
                col_acc[2 + c] = col_lo
            else:
                col_acc[c] += col_hi
                col_acc[2 + c] += col_lo
    for c in range(2):
        for g in range(slots):
            for k in range(block):
                at = site_ref[k]
                p = g * 2 + c
                row = st[p, pl.ds(at, 1), :] + (0.5 * step_size) * sl[p, pl.ds(at, 1), :]
                dest = (c * slots + g) * block + k
                row_pack[dest : dest + 1, :] = row

    def req_wait(i, carry):
        receive(req_ref, req_in, req_send, req_recv, i).wait_recv()
        return carry

    lax.fori_loop(1, tiers, req_wait, 0)
    codes = jnp.transpose(req_in[:, 0, :])
    lane_c = lax.broadcasted_iota(jnp.int32, (cw, sel_c.shape[1]), 1).astype(f32)
    lane_r = lax.broadcasted_iota(jnp.int32, (rw, sel_r.shape[1]), 1).astype(f32)
    for t in range(tiers):
        sel_c[t * cw : (t + 1) * cw, :] = jnp.where(codes[0:cw, t : t + 1] == lane_c, 1.0, 0.0)
        sel_r[t * rw : (t + 1) * rw, :] = jnp.where(
            codes[cw : cw + rw, t : t + 1] == lane_r, 1.0, 0.0
        )
    pick_c = sel_c[...].astype(bf16)
    pick_r = sel_r[...].astype(bf16)
    pack_hi, pack_lo = split(row_pack[...])
    send_r[...] = (mm(pick_r, pack_hi) + mm(pick_r, pack_lo)).reshape(tiers, rw, levels)
    for c in range(2):
        packed = mm_nt(pick_c, col_acc[c].astype(bf16)) + mm_nt(
            pick_c, col_acc[2 + c].astype(bf16)
        )
        send_c[:, :, c * rows : (c + 1) * rows] = packed.reshape(tiers, cw, rows)

    def pack_start(i, carry):
        send(send_r, recv_r, r_send, r_recv, i).start()
        send(send_c, recv_c, c_send, c_recv, i).start()
        return carry

    lax.fori_loop(1, tiers, pack_start, 0)
    recv_c[me] = send_c[me]
    recv_r[me] = send_r[me]

    @pl.when(sy > 0)
    def _():
        for copy in halo(0):
            copy.wait_recv()

    @pl.when(sy < systems - 1)
    def _():
        for copy in halo(1):
            copy.wait_recv()

    neg_hi, neg_lo = split(neg_h_ref[...])
    loc_hi, loc_lo = split(loc_h_ref[...])

    def commute(p):
        hi, lo = z_hi[p], z_lo[p]
        g, c = p // 2, p % 2
        both = mm(loc_hi, hi) + mm(hi, neg_hi)
        both += mm(loc_hi, lo) + mm(hi, neg_lo)
        both += mm(loc_lo, hi) + mm(lo, neg_hi)
        ghost = [halo_st[s, g, c] + (0.5 * step_size) * halo_sl[s, g, c] for s in range(2)]
        extra = mm3(halo_h_ref[...], jnp.concatenate(ghost, axis=0))
        return both, extra

    for g in range(slots):
        for c in range(2):
            both, extra = commute(g * 2 + 1 - c)
            p = g * 2 + c
            sign = 1.0 if c == 0 else -1.0
            mid = st[p] + (0.5 * step_size) * sl[p]
            d_buf[p] = sign * both - damp_ref[g] * mid
            d_buf[p, 0:edge, :] += sign * extra[0:edge]
            d_buf[p, rows - edge : rows, :] += sign * extra[edge : 2 * edge]
            pltpu.make_async_copy(d_buf.at[p], d_hbm.at[g, c], out_sem.at[p]).start()

    def pack_wait(i, carry):
        receive(send_r, recv_r, r_send, r_recv, i).wait_recv()
        receive(send_c, recv_c, c_send, c_recv, i).wait_recv()
        return carry

    lax.fori_loop(1, tiers, pack_wait, 0)
    got_c = recv_c[...].reshape(tiers * cw, 2 * rows)
    got_r = recv_r[...].reshape(tiers * rw, levels)
    r_ref[...] = mm3(mix_r_ref[...], got_r)
    c_ref[...] = mm3(mix_c_ref[0], got_c[:, 0:rows]) + mm3(mix_c_ref[1], got_c[:, rows : 2 * rows])

    def finish(i, carry):
        send(req_ref, req_in, req_send, req_recv, i).wait_send()
        send(send_r, recv_r, r_send, r_recv, i).wait_send()
        send(send_c, recv_c, c_send, c_recv, i).wait_send()
        return carry

    lax.fori_loop(1, tiers, finish, 0)

    @pl.when(sy < systems - 1)
    def _():
        for copy in halo(0):
            copy.wait_send()

    @pl.when(sy > 0)
    def _():
        for copy in halo(1):
            copy.wait_send()

    for p in range(planes):
        pltpu.make_async_copy(d_buf.at[p], d_hbm.at[p // 2, p % 2], out_sem.at[p]).wait()


def finish_kernel(
    live_ref, col_site_ref, row_site_ref, c_ref, r_ref, d_ref, st_ref, sl_ref, next_ref, sum_ref
):
    rows, levels = d_ref.shape[2], d_ref.shape[3]
    wide_m, wide_b = c_ref.shape[0], r_ref.shape[0]
    live = live_ref[pl.program_id(0)]
    lanes = lax.broadcasted_iota(jnp.int32, (wide_m, levels), 1)
    spread = jnp.where(col_site_ref[...] == lanes, 1.0, 0.0).astype(bf16)
    row_lanes = lax.broadcasted_iota(jnp.int32, (wide_b, rows), 1)
    row_at = jnp.where(row_site_ref[...] == row_lanes, 1.0, 0.0)
    col = c_ref[...]
    col_hi = col.astype(bf16).astype(f32)
    left = jnp.concatenate([col_hi, col - col_hi, row_at, row_at], axis=0)
    row_hi, row_lo = split(r_ref[...])
    right = jnp.concatenate([spread, spread, row_hi, row_lo], axis=0)
    added = mm(jnp.transpose(left).astype(bf16), right)
    slope_next = (d_ref[0, 0] + added) * live
    next_ref[0, 0] = slope_next
    sum_ref[0, 0] = (
        st_ref[0, 0] + step_size / 6.0 * sl_ref[0, 0] + step_size / 3.0 * slope_next
    ) * live


def lookup(index, table):
    matches = index[..., None] == jnp.arange(table.shape[-1], dtype=jnp.int32)
    return jnp.sum(jnp.where(matches, table, jnp.zeros((), table.dtype)), axis=-1)


def shards(tiers, systems, state, slope, counts, links, mode_site, mode_coef, mode_rate, h_bands):
    slots, _, rows, levels = state.shape
    edge = h_bands.shape[0] - 1
    modes = mode_site.shape[0]
    block = modes // systems
    per_slot = links.shape[2]
    total = slots * per_slot
    cp = total // tiers
    rp = 2 * -(-(slots * block) // tiers)
    cw, rw = up(cp, 8), up(2 * rp, 8)
    wide_m, wide_b = up(modes, 16), up(block, 16)
    tier_index = lax.axis_index("tier")
    sys_index = lax.axis_index("sys")
    row_start = sys_index * rows

    neighbour = links[0].reshape(-1)
    mode = links[1].reshape(-1)
    downward = links[2].reshape(-1) == 1
    level = links[3].reshape(-1).astype(f32)
    holder = neighbour // slots
    target = neighbour % slots
    in_block = mode // block == sys_index
    local_mode = mode - sys_index * block
    near = (target < lookup(holder, counts)).astype(f32)
    w_re = jnp.where(downward, level * lookup(mode, mode_coef[0]), 1.0) * near
    w_im = jnp.where(downward, level * lookup(mode, mode_coef[1]), 0.0) * near
    rate = jnp.where(downward, level * lookup(mode, mode_rate), 0.0)
    damp = jnp.sum(rate.reshape(slots, per_slot), axis=1)
    order = jnp.arange(total, dtype=jnp.int32)
    same = (holder[:, None] == holder[None, :]) & (order[None, :] < order[:, None])
    rank_c = jnp.sum(same.astype(jnp.int32), axis=1)
    rank_r = jnp.sum((same & in_block[None, :]).astype(jnp.int32), axis=1)

    lane = jnp.arange(128, dtype=jnp.int32)
    here = holder[None, :] == jnp.arange(tiers, dtype=jnp.int32)[:, None]
    code_c = target * modes + mode
    hit = here[:, None, :] & (rank_c[None, None, :] == lane[None, :, None])
    req = jnp.sum(jnp.where(hit, (code_c + 1)[None, None, :], 0), axis=-1)
    for c in range(2):
        hit = (
            here[:, None, :]
            & (in_block & (rank_r < rp))[None, None, :]
            & ((cw + c * rp + rank_r)[None, None, :] == lane[None, :, None])
        )
        code_r = (c * slots + target) * block + local_mode
        req += jnp.sum(jnp.where(hit, (code_r + 1)[None, None, :], 0), axis=-1)
    req = (req - 1).astype(f32).reshape(tiers, 1, 128)

    wide_gm = up(slots * modes, 128)
    lane_gm = jnp.arange(wide_gm, dtype=jnp.int32)
    lane_site = jnp.where(
        lane_gm < slots * modes, jnp.pad(jnp.tile(mode_site, slots), (0, wide_gm - slots * modes)), -1
    )
    lane_info = jnp.stack([lane_site, lane_gm // modes])
    block_sites = lax.dynamic_slice_in_dim(mode_site, sys_index * block, block) - row_start

    slot_of = order // per_slot
    gck = jnp.arange(slots * 2 * wide_m, dtype=jnp.int32)
    g_i, c_i, k_i = gck // (2 * wide_m), gck // wide_m % 2, gck % wide_m
    owns = (g_i[:, None] == slot_of[None, :]) & (k_i[:, None] == mode[None, :])
    at_c = (
        (holder * cw + rank_c)[:, None] == jnp.arange(tiers * cw, dtype=jnp.int32)[None, :]
    ).astype(f32)
    first = (c_i == 0)[:, None]
    coef_from_re = jnp.where(owns, jnp.where(first, w_im[None, :], w_re[None, :]), 0.0)
    coef_from_im = jnp.where(owns, jnp.where(first, -w_re[None, :], w_im[None, :]), 0.0)
    hp = lax.Precision.HIGHEST
    mix_c = jnp.dot(
        jnp.concatenate([coef_from_re, coef_from_im]), at_c, precision=hp
    ).reshape(2, slots * 2 * wide_m, tiers * cw)
    gck = jnp.arange(slots * 2 * wide_b, dtype=jnp.int32)
    g_i, c_i, k_i = gck // (2 * wide_b), gck // wide_b % 2, gck % wide_b
    owns = (
        (g_i[:, None] == slot_of[None, :])
        & (k_i[:, None] == local_mode[None, :])
        & in_block[None, :]
    )
    first = (c_i == 0)[:, None]
    packet_r = jnp.arange(tiers * rw, dtype=jnp.int32)[None, :]
    at_re = ((holder * rw + rank_r)[:, None] == packet_r).astype(f32)
    at_im = ((holder * rw + rp + rank_r)[:, None] == packet_r).astype(f32)
    row_from_re = jnp.where(owns, jnp.where(first, w_im[None, :], -w_re[None, :]), 0.0)
    row_from_im = jnp.where(owns, jnp.where(first, w_re[None, :], w_im[None, :]), 0.0)
    mix_r = jnp.dot(
        jnp.concatenate([row_from_re, row_from_im], axis=1),
        jnp.concatenate([at_re, at_im], axis=0),
        precision=hp,
    )

    i_at = jnp.arange(levels, dtype=jnp.int32)[:, None]
    j_at = jnp.arange(levels, dtype=jnp.int32)[None, :]
    shifted = jnp.pad(h_bands, ((0, 0), (edge, 0)))
    dense = jnp.zeros((levels, levels), f32)
    for o in range(edge + 1):
        dense = jnp.where(i_at - j_at == o, h_bands[o][None, :], dense)
        if o:
            dense = jnp.where(
                j_at - i_at == o, shifted[o, edge - o : edge - o + levels][None, :], dense
            )
    local = lax.dynamic_slice(dense, (row_start, row_start), (rows, rows))
    padded = jnp.pad(dense, ((0, 0), (edge, edge)))
    top = lax.dynamic_slice(padded, (row_start, row_start), (edge, edge))
    bottom = lax.dynamic_slice(
        padded, (row_start + rows - edge, row_start + rows + edge), (edge, edge)
    )
    blank = jnp.zeros((edge, edge), f32)
    halo_h = jnp.concatenate(
        [jnp.concatenate([top, blank], axis=1), jnp.concatenate([blank, bottom], axis=1)], axis=0
    )

    vmem = pl.BlockSpec(memory_space=pltpu.VMEM)
    smem = pl.BlockSpec(memory_space=pltpu.SMEM)
    hbm = pl.BlockSpec(memory_space=pl.ANY)
    planes = slots * 2
    wide_rp = up(2 * slots * block, 128)
    dma = pltpu.SemaphoreType.DMA
    deriv, col_mix, row_mix = pl.pallas_call(
        functools.partial(
            exchange_kernel, (tiers, systems, slots, modes, block, edge, cw, rw)
        ),
        out_shape=(
            jax.ShapeDtypeStruct(state.shape, f32),
            jax.ShapeDtypeStruct((slots * 2 * wide_m, rows), f32),
            jax.ShapeDtypeStruct((slots * 2 * wide_b, levels), f32),
        ),
        in_specs=[vmem, vmem, smem, smem, vmem, vmem, vmem, vmem, vmem, hbm, hbm],
        out_specs=(hbm, vmem, vmem),
        scratch_shapes=[
            pltpu.VMEM((planes, rows, levels), f32),
            pltpu.VMEM((planes, rows, levels), f32),
            pltpu.VMEM((planes, rows, levels), bf16),
            pltpu.VMEM((planes, rows, levels), bf16),
            pltpu.VMEM((planes, rows, levels), f32),
            pltpu.VMEM((tiers, 1, 128), f32),
            pltpu.VMEM((2, slots, 2, edge, levels), f32),
            pltpu.VMEM((2, slots, 2, edge, levels), f32),
            pltpu.VMEM((4, rows, wide_gm), f32),
            pltpu.VMEM((wide_rp, levels), f32),
            pltpu.VMEM((tiers * cw, wide_gm), f32),
            pltpu.VMEM((tiers * rw, wide_rp), f32),
            pltpu.VMEM((tiers, cw, 2 * rows), f32),
            pltpu.VMEM((tiers, rw, levels), f32),
            pltpu.VMEM((tiers, cw, 2 * rows), f32),
            pltpu.VMEM((tiers, rw, levels), f32),
            dma((2, planes)),
            dma((planes,)),
            dma((tiers,)),
            dma((tiers,)),
            dma((2, 2)),
            dma((2, 2)),
            dma((tiers,)),
            dma((tiers,)),
            dma((tiers,)),
            dma((tiers,)),
        ],
        compiler_params=pltpu.CompilerParams(collective_id=0, has_side_effects=True),
        name="exchange",
    )(req, lane_info, block_sites, damp, -dense, local, halo_h, mix_c, mix_r, state, slope)

    live = (jnp.arange(slots, dtype=jnp.int32) < lookup(tier_index, counts)).astype(f32)
    col_site = jnp.pad(mode_site, (0, wide_m - modes), constant_values=-1)[:, None]
    row_site = jnp.pad(block_sites, (0, wide_b - block), constant_values=-1)[:, None]
    plane = pl.BlockSpec((1, 1, rows, levels), lambda g, c: (g, c, 0, 0))
    fixed = lambda g, c: (0, 0)
    mixed = lambda g, c: (g * 2 + c, 0)
    return pl.pallas_call(
        finish_kernel,
        grid=(slots, 2),
        out_shape=(jax.ShapeDtypeStruct(state.shape, f32),) * 2,
        in_specs=[
            smem,
            pl.BlockSpec((wide_m, 1), fixed),
            pl.BlockSpec((wide_b, 1), fixed),
            pl.BlockSpec((wide_m, rows), mixed),
            pl.BlockSpec((wide_b, levels), mixed),
            plane,
            plane,
            plane,
        ],
        out_specs=(plane, plane),
        name="finish",
    )(live, col_site, row_site, col_mix, row_mix, deriv, state, slope)


def solution(mesh):
    in_specs = (
        P("tier", None, "sys", None),
        P("tier", None, "sys", None),
        P(),
        P(None, "tier", None),
        P(),
        P(),
        P(),
        P(),
    )
    out_specs = (P("tier", None, "sys", None), P("tier", None, "sys", None))
    body = functools.partial(shards, mesh.shape["tier"], mesh.shape["sys"])
    return jax.shard_map(body, mesh=mesh, in_specs=in_specs, out_specs=out_specs, check_vma=False)
```

```python
import functools

import jax
import jax.numpy as jnp
from jax import lax
from jax.experimental import pallas as pl
from jax.experimental.pallas import tpu as pltpu
from jax.sharding import PartitionSpec as P

step_size = 0.05
MESH = pl.DeviceIdType.MESH
f32 = jnp.float32
bf16 = jnp.bfloat16


def up(value, unit):
    return (value + unit - 1) // unit * unit


def split(value):
    hi = value.astype(bf16)
    lo = (value - hi.astype(f32)).astype(bf16)
    return hi, lo


def mm(a, b):
    return lax.dot_general(a, b, (((1,), (0,)), ((), ())), preferred_element_type=f32)


def mm_nt(a, b):
    return lax.dot_general(a, b, (((1,), (1,)), ((), ())), preferred_element_type=f32)


def mm3(a, b):
    a_hi, a_lo = split(a)
    b_hi, b_lo = split(b)
    return mm(a_hi, b_hi) + (mm(a_hi, b_lo) + mm(a_lo, b_hi))


def banded(diff, bands, edge):
    total = jnp.where(diff == 0, bands[0:1, :], 0.0)
    for o in range(1, edge + 1):
        total = jnp.where(diff == o, bands[o : o + 1, :], total)
        total = jnp.where(diff == -o, pltpu.roll(bands, o, 1)[o : o + 1, :], total)
    return total


def exchange_kernel(
    dims,
    links_ref,
    counts_ref,
    site_ref,
    coef_ref,
    rate_ref,
    bands_ref,
    state_hbm,
    slope_hbm,
    d_buf,
    base_ref,
    c_ref,
    r_ref,
    spread_ref,
    row_at_ref,
    st,
    sl,
    z_hi,
    z_lo,
    h_hi,
    h_lo,
    bands_pad,
    req_ref,
    req_in,
    halo_st,
    halo_sl,
    col_acc,
    row_pack,
    sel_c,
    sel_r,
    send_c,
    send_r,
    recv_c,
    recv_r,
    load_sem,
    req_send,
    req_recv,
    halo_send,
    halo_recv,
    c_send,
    c_recv,
    r_send,
    r_recv,
):
    tiers, systems, slots, modes, block, edge, per_slot, rp, cw, rw = dims
    rows, levels = st.shape[1], st.shape[2]
    me = lax.axis_index("tier")
    sy = lax.axis_index("sys")
    planes = slots * 2

    def load(p):
        g, c = p // 2, p % 2
        return (
            pltpu.make_async_copy(state_hbm.at[g, c], st.at[p], load_sem.at[0, p]),
            pltpu.make_async_copy(slope_hbm.at[g, c], sl.at[p], load_sem.at[1, p]),
        )

    for p in range(planes):
        for copy in load(p):
            copy.start()

    barrier = pltpu.get_barrier_semaphore()

    def greet(i, carry):
        pl.semaphore_signal(
            barrier, inc=1, device_id=(lax.rem(me + i, tiers), sy), device_id_type=MESH
        )
        return carry

    lax.fori_loop(1, tiers, greet, 0)

    @pl.when(sy > 0)
    def _():
        pl.semaphore_signal(barrier, inc=1, device_id=(me, sy - 1), device_id_type=MESH)

    @pl.when(sy < systems - 1)
    def _():
        pl.semaphore_signal(barrier, inc=1, device_id=(me, sy + 1), device_id_type=MESH)

    total = slots * per_slot
    wide_q = up(total, 128)

    def iota(shape, axis):
        return lax.broadcasted_iota(jnp.int32, shape, axis).astype(f32)

    def flag(where):
        return jnp.where(where, 1.0, 0.0)

    flat = jnp.zeros((4, wide_q), f32)
    for g in range(slots):
        place = flag(
            iota((per_slot, wide_q), 1) == iota((per_slot, wide_q), 0) + float(g * per_slot)
        )
        flat += mm(links_ref[:, g, :].astype(f32).astype(bf16), place.astype(bf16))
    lane_q = iota((1, wide_q), 1)
    valid = lane_q < float(total)
    mode, kind, level = flat[1:2], flat[2:3], flat[3:4]
    holder = jnp.floor((flat[0:1] + 0.5) * (1.0 / slots))
    target = flat[0:1] - holder * float(slots)
    holder = jnp.where(valid, holder, -1.0)
    slot_of = jnp.where(valid, jnp.floor((lane_q + 0.5) * (1.0 / per_slot)), -1.0)
    first_mode = (sy * block).astype(f32)
    in_block = valid & (mode >= first_mode) & (mode < first_mode + float(block))
    local_mode = mode - first_mode
    has = flag(holder == iota((tiers, wide_q), 0))
    has_r = has * flag(in_block)
    before = flag(iota((wide_q, wide_q), 0) < iota((wide_q, wide_q), 1)).astype(bf16)
    rank_c = jnp.sum(has * mm(has.astype(bf16), before), axis=0, keepdims=True)
    rank_r = jnp.sum(has_r * mm(has_r.astype(bf16), before), axis=0, keepdims=True)
    lane_j = iota((128, wide_q), 0)

    def asked(codes, ranks):
        return mm_nt(codes.astype(bf16), flag(lane_j == ranks).astype(bf16))

    req = asked(has * (target * float(modes) + mode + 1.0), rank_c) - 1.0
    for c in range(2):
        code = (target + float(c * slots)) * float(block) + local_mode + 1.0
        req += asked(has_r * code, rank_r + float(cw + c * rp))
    for t in range(tiers):
        req_ref[t] = req[t : t + 1, :]

    inner = (sy > 0).astype(jnp.int32) + (sy < systems - 1).astype(jnp.int32)
    pl.semaphore_wait(barrier, tiers - 1 + inner)

    def send(src, dst, send_sem, recv_sem, i):
        peer = lax.rem(me + i, tiers)
        return pltpu.make_async_remote_copy(
            src_ref=src.at[peer],
            dst_ref=dst.at[me],
            send_sem=send_sem.at[i],
            recv_sem=recv_sem.at[i],
            device_id=(peer, sy),
            device_id_type=MESH,
        )

    def receive(src, dst, send_sem, recv_sem, i):
        peer = lax.rem(me + tiers - i, tiers)
        return pltpu.make_async_remote_copy(
            src_ref=src.at[peer],
            dst_ref=dst.at[peer],
            send_sem=send_sem.at[i],
            recv_sem=recv_sem.at[i],
            device_id=(peer, sy),
            device_id_type=MESH,
        )

    def req_start(i, carry):
        send(req_ref, req_in, req_send, req_recv, i).start()
        return carry

    lax.fori_loop(1, tiers, req_start, 0)

    def halo(side):
        first = rows - edge if side == 0 else 0
        target = sy + 1 if side == 0 else sy - 1
        return [
            pltpu.make_async_remote_copy(
                src_ref=src.at[:, :, pl.ds(first, edge), :],
                dst_ref=dst.at[side],
                send_sem=halo_send.at[side, n],
                recv_sem=halo_recv.at[side, n],
                device_id=(me, target),
                device_id_type=MESH,
            )
            for n, (src, dst) in enumerate(((state_hbm, halo_st), (slope_hbm, halo_sl)))
        ]

    @pl.when(sy < systems - 1)
    def _():
        for copy in halo(0):
            copy.start()

    @pl.when(sy > 0)
    def _():
        for copy in halo(1):
            copy.start()

    @pl.when(sy == 0)
    def _():
        halo_st[0] = jnp.zeros_like(halo_st[0])
        halo_sl[0] = jnp.zeros_like(halo_sl[0])

    @pl.when(sy == systems - 1)
    def _():
        halo_st[1] = jnp.zeros_like(halo_st[1])
        halo_sl[1] = jnp.zeros_like(halo_sl[1])

    req_in[me] = req_ref[me]
    row_pack[...] = jnp.zeros_like(row_pack)
    width = col_acc.shape[-1]
    lane_gm = iota((1, width), 1)
    lane_slot = jnp.floor((lane_gm + 0.5) * (1.0 / modes))
    lane_mode = lane_gm - lane_slot * float(modes)
    lane_site = jnp.zeros((1, width), jnp.int32)
    for k in range(modes):
        lane_site = jnp.where(lane_mode == float(k), site_ref[k], lane_site)
    level_at = lax.broadcasted_iota(jnp.int32, (levels, width), 0)
    for g in range(slots):
        pick = jnp.where((level_at == lane_site) & (lane_slot == float(g)), 1.0, 0.0).astype(bf16)
        for c in range(2):
            p = g * 2 + c
            for copy in load(p):
                copy.wait()
            hi, lo = split(st[p] + (0.5 * step_size) * sl[p])
            z_hi[p] = hi
            z_lo[p] = lo
            col_hi = mm(hi, pick)
            col_lo = mm(lo, pick)
            if g == 0:
                col_acc[c] = col_hi
                col_acc[2 + c] = col_lo
            else:
                col_acc[c] += col_hi
                col_acc[2 + c] += col_lo
    for c in range(2):
        for g in range(slots):
            for k in range(block):
                at = jnp.clip(site_ref[sy * block + k] - sy * rows, 0, rows - 1)
                p = g * 2 + c
                row = st[p, pl.ds(at, 1), :] + (0.5 * step_size) * sl[p, pl.ds(at, 1), :]
                dest = (c * slots + g) * block + k
                row_pack[dest : dest + 1, :] = row

    row_start = sy * rows
    bands_pad[...] = jnp.zeros_like(bands_pad)
    bands_pad[0 : edge + 1, :] = bands_ref[...]
    bands = bands_pad[...]
    strip = min(128, levels)

    def dense(i, carry):
        at = pl.multiple_of(i * strip, strip)
        diff = (
            lax.broadcasted_iota(jnp.int32, (strip, levels), 0)
            + at
            - lax.broadcasted_iota(jnp.int32, (strip, levels), 1)
        )
        hi, lo = split(-banded(diff, bands, edge))
        h_hi[pl.ds(at, strip), :] = hi
        h_lo[pl.ds(at, strip), :] = lo
        return carry

    lax.fori_loop(0, levels // strip, dense, 0)

    def rolled(shift):
        return pltpu.roll(bands, lax.rem(shift + 2 * levels, levels), 1)

    wide_r = up(rows, 128)
    diff = lax.broadcasted_iota(jnp.int32, (rows, wide_r), 0) - lax.broadcasted_iota(
        jnp.int32, (rows, wide_r), 1
    )
    near_bands = rolled(-row_start)
    loc = jnp.where(diff == 0, near_bands[0:1, :wide_r], 0.0)
    for o in range(1, edge + 1):
        loc = jnp.where(diff == o, near_bands[o : o + 1, :wide_r], loc)
        loc = jnp.where(diff == -o, pltpu.roll(near_bands, o, 1)[o : o + 1, :wide_r], loc)
    loc_hi, loc_lo = split(loc[:, :rows])
    sub = lax.broadcasted_iota(jnp.int32, (2 * edge, 128), 0)
    lan = lax.broadcasted_iota(jnp.int32, (2 * edge, 128), 1)
    low_bands = rolled(edge - row_start)
    high_bands = rolled(edge - row_start - rows)
    halo_h = jnp.zeros((2 * edge, 128), f32)
    for o in range(edge + 1):
        low = (sub < edge) & (lan < edge) & (edge + sub - lan == o)
        high = (sub >= edge) & (lan >= edge) & (lan < 2 * edge) & (edge + lan - sub == o)
        above = pltpu.roll(high_bands, o, 1) if o else high_bands
        halo_h = jnp.where(low, low_bands[o : o + 1, :128], halo_h)
        halo_h = jnp.where(high, above[o : o + 1, :128], halo_h)
    halo_h = halo_h[:, : 2 * edge]

    def req_wait(i, carry):
        receive(req_ref, req_in, req_send, req_recv, i).wait_recv()
        return carry

    lax.fori_loop(1, tiers, req_wait, 0)
    codes = jnp.transpose(req_in[:, 0, :])
    lane_c = lax.broadcasted_iota(jnp.int32, (cw, sel_c.shape[1]), 1).astype(f32)
    lane_r = lax.broadcasted_iota(jnp.int32, (rw, sel_r.shape[1]), 1).astype(f32)
    for t in range(tiers):
        sel_c[t * cw : (t + 1) * cw, :] = jnp.where(codes[0:cw, t : t + 1] == lane_c, 1.0, 0.0)
        sel_r[t * rw : (t + 1) * rw, :] = jnp.where(
            codes[cw : cw + rw, t : t + 1] == lane_r, 1.0, 0.0
        )
    pick_c = sel_c[...].astype(bf16)
    pick_r = sel_r[...].astype(bf16)
    pack_hi, pack_lo = split(row_pack[...])
    send_r[...] = (mm(pick_r, pack_hi) + mm(pick_r, pack_lo)).reshape(tiers, rw, levels)
    for c in range(2):
        packed = mm_nt(pick_c, col_acc[c].astype(bf16)) + mm_nt(
            pick_c, col_acc[2 + c].astype(bf16)
        )
        send_c[:, :, c * rows : (c + 1) * rows] = packed.reshape(tiers, cw, rows)

    def pack_start(i, carry):
        send(send_r, recv_r, r_send, r_recv, i).start()
        send(send_c, recv_c, c_send, c_recv, i).start()
        return carry

    lax.fori_loop(1, tiers, pack_start, 0)
    recv_c[me] = send_c[me]
    recv_r[me] = send_r[me]

    @pl.when(sy > 0)
    def _():
        for copy in halo(0):
            copy.wait_recv()

    @pl.when(sy < systems - 1)
    def _():
        for copy in halo(1):
            copy.wait_recv()

    def table(ref, count, index):
        value = jnp.zeros((1, wide_q), f32)
        for k in range(count):
            value = jnp.where(index == float(k), ref(k), value)
        return value

    own_count = counts_ref[me].astype(f32)
    near = flag(target < table(lambda k: counts_ref[k].astype(f32), tiers, holder))
    near = near * flag(slot_of < own_count)
    down = kind == 1.0
    w_re = jnp.where(down, level * table(lambda k: coef_ref[0, k], modes, mode), 1.0) * near
    w_im = jnp.where(down, level * table(lambda k: coef_ref[1, k], modes, mode), 0.0) * near
    rate = jnp.where(down, level * table(lambda k: rate_ref[k], modes, mode), 0.0)
    wide_m, wide_b = spread_ref.shape[0], row_at_ref.shape[0]

    def mixing(wide, index, mask, signs):
        from_re, from_im = [], []
        for g in range(slots):
            own = flag((iota((wide, wide_q), 0) == index) & (slot_of == float(g)) & mask)
            for re, im in signs:
                from_re.append(own * re)
                from_im.append(own * im)
        return jnp.concatenate(from_re, axis=0), jnp.concatenate(from_im, axis=0)

    def packets(count, at, mask):
        return flag((iota((count, wide_q), 0) == at) & mask).astype(bf16)

    def place(value, at):
        hi, lo = split(value)
        return mm_nt(hi, at) + mm_nt(lo, at)

    at_c = packets(tiers * cw, holder * float(cw) + rank_c, valid)
    from_re, from_im = mixing(wide_m, mode, valid, ((w_im, -w_re), (w_re, w_im)))
    mix_c = (place(from_re, at_c), place(from_im, at_c))
    from_re, from_im = mixing(wide_b, local_mode, in_block, ((w_im, w_re), (-w_re, w_im)))
    at_row = holder * float(rw) + rank_r
    mix_r = place(from_re, packets(tiers * rw, at_row, in_block)) + place(
        from_im, packets(tiers * rw, at_row + float(rp), in_block)
    )
    site_lane = lax.broadcasted_iota(jnp.int32, (1, levels), 1)
    spread_ref[...] = jnp.zeros_like(spread_ref)
    for k in range(modes):
        spread_ref[k : k + 1, :] = flag(site_lane == site_ref[k])
    row_lane = lax.broadcasted_iota(jnp.int32, (1, rows), 1)
    row_at_ref[...] = jnp.zeros_like(row_at_ref)
    for k in range(block):
        row_at_ref[k : k + 1, :] = flag(row_lane == site_ref[sy * block + k] - row_start)

    def commute(p):
        hi, lo = z_hi[p], z_lo[p]
        g, c = p // 2, p % 2
        neg_hi = h_hi[...]
        both = mm(loc_hi, hi) + mm(hi, neg_hi)
        both += mm(loc_hi, lo) + mm(hi, h_lo[...])
        both += mm(loc_lo, hi) + mm(lo, neg_hi)
        ghost = [halo_st[s, g, c] + (0.5 * step_size) * halo_sl[s, g, c] for s in range(2)]
        extra = mm3(halo_h, jnp.concatenate(ghost, axis=0))
        return both, extra

    for g in range(slots):
        live = flag(own_count > float(g))
        damp = jnp.sum(jnp.where(slot_of == float(g), rate, 0.0), axis=1, keepdims=True) * live
        for c in range(2):
            both, extra = commute(g * 2 + 1 - c)
            p = g * 2 + c
            sign = live if c == 0 else -live
            mid = st[p] + (0.5 * step_size) * sl[p]
            d_buf[p] = sign * both - damp * mid
            d_buf[p, 0:edge, :] += sign * extra[0:edge]
            d_buf[p, rows - edge : rows, :] += sign * extra[edge : 2 * edge]
            base_ref[p] = live * (st[p] + (step_size / 6.0) * sl[p])

    def pack_wait(i, carry):
        receive(send_r, recv_r, r_send, r_recv, i).wait_recv()
        receive(send_c, recv_c, c_send, c_recv, i).wait_recv()
        return carry

    lax.fori_loop(1, tiers, pack_wait, 0)
    got_c = recv_c[...].reshape(tiers * cw, 2 * rows)
    got_r = recv_r[...].reshape(tiers * rw, levels)
    r_ref[...] = mm3(mix_r, got_r)
    c_ref[...] = mm3(mix_c[0], got_c[:, 0:rows]) + mm3(mix_c[1], got_c[:, rows : 2 * rows])

    def finish(i, carry):
        send(req_ref, req_in, req_send, req_recv, i).wait_send()
        send(send_r, recv_r, r_send, r_recv, i).wait_send()
        send(send_c, recv_c, c_send, c_recv, i).wait_send()
        return carry

    lax.fori_loop(1, tiers, finish, 0)

    @pl.when(sy < systems - 1)
    def _():
        for copy in halo(0):
            copy.wait_send()

    @pl.when(sy > 0)
    def _():
        for copy in halo(1):
            copy.wait_send()


def finish_kernel(spread_ref, row_at_ref, c_ref, r_ref, d_ref, base_ref, next_ref, sum_ref):
    p = pl.program_id(0)
    spread = spread_ref[...].astype(bf16)
    row_at = row_at_ref[...]
    wide_m, wide_b = spread_ref.shape[0], row_at_ref.shape[0]
    col = c_ref[pl.ds(pl.multiple_of(p * wide_m, wide_m), wide_m), :]
    col_hi = col.astype(bf16).astype(f32)
    left = jnp.concatenate([col_hi, col - col_hi, row_at, row_at], axis=0)
    row_hi, row_lo = split(r_ref[pl.ds(pl.multiple_of(p * wide_b, wide_b), wide_b), :])
    right = jnp.concatenate([spread, spread, row_hi, row_lo], axis=0)
    slope_next = d_ref[p] + mm(jnp.transpose(left).astype(bf16), right)
    next_ref[0] = slope_next
    sum_ref[0] = base_ref[p] + step_size / 3.0 * slope_next


def shards(tiers, systems, state, slope, counts, links, mode_site, mode_coef, mode_rate, h_bands):
    slots, _, rows, levels = state.shape
    edge = h_bands.shape[0] - 1
    modes = mode_site.shape[0]
    block = modes // systems
    per_slot = links.shape[2]
    total = slots * per_slot
    cp = total // tiers
    rp = 2 * -(-(slots * block) // tiers)
    cw, rw = up(cp, 8), up(2 * rp, 8)
    wide_m, wide_b = up(modes, 16), up(block, 16)
    vmem = pl.BlockSpec(memory_space=pltpu.VMEM)
    smem = pl.BlockSpec(memory_space=pltpu.SMEM)
    hbm = pl.BlockSpec(memory_space=pl.ANY)
    planes = slots * 2
    wide_gm = up(slots * modes, 128)
    wide_rp = up(2 * slots * block, 128)
    dma = pltpu.SemaphoreType.DMA
    big = (planes, rows, levels)
    deriv, base, col_mix, row_mix, spread, row_at = pl.pallas_call(
        functools.partial(
            exchange_kernel, (tiers, systems, slots, modes, block, edge, per_slot, rp, cw, rw)
        ),
        out_shape=(
            pltpu.VMEM(big, f32),
            pltpu.VMEM(big, f32),
            pltpu.VMEM((planes * wide_m, rows), f32),
            pltpu.VMEM((planes * wide_b, levels), f32),
            pltpu.VMEM((wide_m, levels), f32),
            pltpu.VMEM((wide_b, rows), f32),
        ),
        in_specs=[vmem, smem, smem, smem, smem, vmem, hbm, hbm],
        out_specs=(vmem,) * 6,
        scratch_shapes=[
            pltpu.VMEM((planes, rows, levels), f32),
            pltpu.VMEM((planes, rows, levels), f32),
            pltpu.VMEM((planes, rows, levels), bf16),
            pltpu.VMEM((planes, rows, levels), bf16),
            pltpu.VMEM((levels, levels), bf16),
            pltpu.VMEM((levels, levels), bf16),
            pltpu.VMEM((up(edge + 1, 8), levels), f32),
            pltpu.VMEM((tiers, 1, 128), f32),
            pltpu.VMEM((tiers, 1, 128), f32),
            pltpu.VMEM((2, slots, 2, edge, levels), f32),
            pltpu.VMEM((2, slots, 2, edge, levels), f32),
            pltpu.VMEM((4, rows, wide_gm), f32),
            pltpu.VMEM((wide_rp, levels), f32),
            pltpu.VMEM((tiers * cw, wide_gm), f32),
            pltpu.VMEM((tiers * rw, wide_rp), f32),
            pltpu.VMEM((tiers, cw, 2 * rows), f32),
            pltpu.VMEM((tiers, rw, levels), f32),
            pltpu.VMEM((tiers, cw, 2 * rows), f32),
            pltpu.VMEM((tiers, rw, levels), f32),
            dma((2, planes)),
            dma((tiers,)),
            dma((tiers,)),
            dma((2, 2)),
            dma((2, 2)),
            dma((tiers,)),
            dma((tiers,)),
            dma((tiers,)),
            dma((tiers,)),
        ],
        compiler_params=pltpu.CompilerParams(
            collective_id=0, has_side_effects=True, vmem_limit_bytes=32 << 20
        ),
        name="exchange",
    )(links, counts, mode_site, mode_coef, mode_rate, h_bands, state, slope)
    plane = pl.BlockSpec((1, rows, levels), lambda p: (p, 0, 0))
    outs = pl.pallas_call(
        finish_kernel,
        grid=(planes,),
        out_shape=(jax.ShapeDtypeStruct(big, f32),) * 2,
        in_specs=[vmem] * 6,
        out_specs=(plane, plane),
        compiler_params=pltpu.CompilerParams(vmem_limit_bytes=16 << 20),
        name="finish",
    )(spread, row_at, col_mix, row_mix, deriv, base)
    return tuple(out.reshape(state.shape) for out in outs)


def solution(mesh):
    in_specs = (
        P("tier", None, "sys", None),
        P("tier", None, "sys", None),
        P(),
        P(None, "tier", None),
        P(),
        P(),
        P(),
        P(),
    )
    out_specs = (P("tier", None, "sys", None), P("tier", None, "sys", None))
    body = functools.partial(shards, mesh.shape["tier"], mesh.shape["sys"])
    return jax.shard_map(body, mesh=mesh, in_specs=in_specs, out_specs=out_specs, check_vma=False)
```

```python
import functools

import jax
import jax.numpy as jnp
from jax import lax
from jax.experimental import pallas as pl
from jax.experimental.pallas import tpu as pltpu
from jax.sharding import PartitionSpec as P

step_size = 0.05
MESH = pl.DeviceIdType.MESH
f32 = jnp.float32
bf16 = jnp.bfloat16


def up(value, unit):
    return (value + unit - 1) // unit * unit


def split(value):
    hi = value.astype(bf16)
    lo = (value - hi.astype(f32)).astype(bf16)
    return hi, lo


def mm(a, b):
    return lax.dot_general(a, b, (((1,), (0,)), ((), ())), preferred_element_type=f32)


def mm_nt(a, b):
    return lax.dot_general(a, b, (((1,), (1,)), ((), ())), preferred_element_type=f32)


def mm3(a, b):
    a_hi, a_lo = split(a)
    b_hi, b_lo = split(b)
    return mm(a_hi, b_hi) + (mm(a_hi, b_lo) + mm(a_lo, b_hi))


def banded(diff, bands, edge):
    total = jnp.where(diff == 0, bands[0:1, :], 0.0)
    for o in range(1, edge + 1):
        total = jnp.where(diff == o, bands[o : o + 1, :], total)
        total = jnp.where(diff == -o, pltpu.roll(bands, o, 1)[o : o + 1, :], total)
    return total


def exchange_kernel(
    dims,
    links_hbm,
    counts_hbm,
    site_hbm,
    coef_hbm,
    rate_hbm,
    bands_hbm,
    state_hbm,
    slope_hbm,
    d_buf,
    base_ref,
    c_ref,
    r_ref,
    spread_ref,
    row_at_ref,
    links_ref,
    counts_ref,
    site_ref,
    coef_ref,
    rate_ref,
    bands_ref,
    st,
    sl,
    z_hi,
    z_lo,
    h_hi,
    h_lo,
    bands_pad,
    req_ref,
    req_in,
    halo_st,
    halo_sl,
    col_acc,
    row_pack,
    sel_c,
    sel_r,
    send_c,
    send_r,
    recv_c,
    recv_r,
    load_sem,
    req_send,
    req_recv,
    halo_send,
    halo_recv,
    c_send,
    c_recv,
    r_send,
    r_recv,
    small_sem,
):
    tiers, systems, slots, modes, block, edge, per_slot, rp, cw, rw = dims
    rows, levels = st.shape[1], st.shape[2]
    me = lax.axis_index("tier")
    sy = lax.axis_index("sys")
    planes = slots * 2

    def load(p):
        g, c = p // 2, p % 2
        return (
            pltpu.make_async_copy(state_hbm.at[g, c], st.at[p], load_sem.at[0, p]),
            pltpu.make_async_copy(slope_hbm.at[g, c], sl.at[p], load_sem.at[1, p]),
        )

    small = [
        pltpu.make_async_copy(src, dst, small_sem.at[n])
        for n, (src, dst) in enumerate(
            (
                (links_hbm, links_ref),
                (counts_hbm, counts_ref),
                (site_hbm, site_ref),
                (coef_hbm, coef_ref),
                (rate_hbm, rate_ref),
                (bands_hbm, bands_ref),
            )
        )
    ]
    for copy in small:
        copy.start()
    for p in range(planes):
        for copy in load(p):
            copy.start()

    barrier = pltpu.get_barrier_semaphore()

    def greet(i, carry):
        pl.semaphore_signal(
            barrier, inc=1, device_id=(lax.rem(me + i, tiers), sy), device_id_type=MESH
        )
        return carry

    lax.fori_loop(1, tiers, greet, 0)

    @pl.when(sy > 0)
    def _():
        pl.semaphore_signal(barrier, inc=1, device_id=(me, sy - 1), device_id_type=MESH)

    @pl.when(sy < systems - 1)
    def _():
        pl.semaphore_signal(barrier, inc=1, device_id=(me, sy + 1), device_id_type=MESH)

    total = slots * per_slot
    wide_q = up(total, 128)

    def iota(shape, axis):
        return lax.broadcasted_iota(jnp.int32, shape, axis).astype(f32)

    def flag(where):
        return jnp.where(where, 1.0, 0.0)

    for copy in small:
        copy.wait()
    flat = jnp.zeros((4, wide_q), f32)
    for g in range(slots):
        place = flag(
            iota((per_slot, wide_q), 1) == iota((per_slot, wide_q), 0) + float(g * per_slot)
        )
        flat += mm(links_ref[:, g, :].astype(f32).astype(bf16), place.astype(bf16))
    lane_q = iota((1, wide_q), 1)
    valid = lane_q < float(total)
    mode, kind, level = flat[1:2], flat[2:3], flat[3:4]
    holder = jnp.floor((flat[0:1] + 0.5) * (1.0 / slots))
    target = flat[0:1] - holder * float(slots)
    holder = jnp.where(valid, holder, -1.0)
    slot_of = jnp.where(valid, jnp.floor((lane_q + 0.5) * (1.0 / per_slot)), -1.0)
    first_mode = (sy * block).astype(f32)
    in_block = valid & (mode >= first_mode) & (mode < first_mode + float(block))
    local_mode = mode - first_mode
    has = flag(holder == iota((tiers, wide_q), 0))
    has_r = has * flag(in_block)
    before = flag(iota((wide_q, wide_q), 0) < iota((wide_q, wide_q), 1)).astype(bf16)
    rank_c = jnp.sum(has * mm(has.astype(bf16), before), axis=0, keepdims=True)
    rank_r = jnp.sum(has_r * mm(has_r.astype(bf16), before), axis=0, keepdims=True)
    lane_j = iota((128, wide_q), 0)

    def asked(codes, ranks):
        return mm_nt(codes.astype(bf16), flag(lane_j == ranks).astype(bf16))

    req = asked(has * (target * float(modes) + mode + 1.0), rank_c) - 1.0
    for c in range(2):
        code = (target + float(c * slots)) * float(block) + local_mode + 1.0
        req += asked(has_r * code, rank_r + float(cw + c * rp))
    for t in range(tiers):
        req_ref[t] = req[t : t + 1, :]

    inner = (sy > 0).astype(jnp.int32) + (sy < systems - 1).astype(jnp.int32)
    pl.semaphore_wait(barrier, tiers - 1 + inner)

    def send(src, dst, send_sem, recv_sem, i):
        peer = lax.rem(me + i, tiers)
        return pltpu.make_async_remote_copy(
            src_ref=src.at[peer],
            dst_ref=dst.at[me],
            send_sem=send_sem.at[i],
            recv_sem=recv_sem.at[i],
            device_id=(peer, sy),
            device_id_type=MESH,
        )

    def receive(src, dst, send_sem, recv_sem, i):
        peer = lax.rem(me + tiers - i, tiers)
        return pltpu.make_async_remote_copy(
            src_ref=src.at[peer],
            dst_ref=dst.at[peer],
            send_sem=send_sem.at[i],
            recv_sem=recv_sem.at[i],
            device_id=(peer, sy),
            device_id_type=MESH,
        )

    def req_start(i, carry):
        send(req_ref, req_in, req_send, req_recv, i).start()
        return carry

    lax.fori_loop(1, tiers, req_start, 0)

    def halo(side):
        first = rows - edge if side == 0 else 0
        target = sy + 1 if side == 0 else sy - 1
        return [
            pltpu.make_async_remote_copy(
                src_ref=src.at[:, :, pl.ds(first, edge), :],
                dst_ref=dst.at[side],
                send_sem=halo_send.at[side, n],
                recv_sem=halo_recv.at[side, n],
                device_id=(me, target),
                device_id_type=MESH,
            )
            for n, (src, dst) in enumerate(((state_hbm, halo_st), (slope_hbm, halo_sl)))
        ]

    @pl.when(sy < systems - 1)
    def _():
        for copy in halo(0):
            copy.start()

    @pl.when(sy > 0)
    def _():
        for copy in halo(1):
            copy.start()

    @pl.when(sy == 0)
    def _():
        halo_st[0] = jnp.zeros_like(halo_st[0])
        halo_sl[0] = jnp.zeros_like(halo_sl[0])

    @pl.when(sy == systems - 1)
    def _():
        halo_st[1] = jnp.zeros_like(halo_st[1])
        halo_sl[1] = jnp.zeros_like(halo_sl[1])

    req_in[me] = req_ref[me]
    row_pack[...] = jnp.zeros_like(row_pack)
    width = col_acc.shape[-1]
    lane_gm = iota((1, width), 1)
    lane_slot = jnp.floor((lane_gm + 0.5) * (1.0 / modes))
    lane_mode = lane_gm - lane_slot * float(modes)
    lane_site = jnp.zeros((1, width), jnp.int32)
    for k in range(modes):
        lane_site = jnp.where(lane_mode == float(k), site_ref[k], lane_site)
    level_at = lax.broadcasted_iota(jnp.int32, (levels, width), 0)
    for g in range(slots):
        pick = jnp.where((level_at == lane_site) & (lane_slot == float(g)), 1.0, 0.0).astype(bf16)
        for c in range(2):
            p = g * 2 + c
            for copy in load(p):
                copy.wait()
            hi, lo = split(st[p] + (0.5 * step_size) * sl[p])
            z_hi[p] = hi
            z_lo[p] = lo
            col_hi = mm(hi, pick)
            col_lo = mm(lo, pick)
            if g == 0:
                col_acc[c] = col_hi
                col_acc[2 + c] = col_lo
            else:
                col_acc[c] += col_hi
                col_acc[2 + c] += col_lo
    for c in range(2):
        for g in range(slots):
            for k in range(block):
                at = jnp.clip(site_ref[sy * block + k] - sy * rows, 0, rows - 1)
                p = g * 2 + c
                row = st[p, pl.ds(at, 1), :] + (0.5 * step_size) * sl[p, pl.ds(at, 1), :]
                dest = (c * slots + g) * block + k
                row_pack[dest : dest + 1, :] = row

    row_start = sy * rows
    bands_pad[...] = jnp.zeros_like(bands_pad)
    bands_pad[0 : edge + 1, :] = bands_ref[...]
    bands = bands_pad[...]
    strip = min(128, levels)

    def dense(i, carry):
        at = pl.multiple_of(i * strip, strip)
        diff = (
            lax.broadcasted_iota(jnp.int32, (strip, levels), 0)
            + at
            - lax.broadcasted_iota(jnp.int32, (strip, levels), 1)
        )
        hi, lo = split(-banded(diff, bands, edge))
        h_hi[pl.ds(at, strip), :] = hi
        h_lo[pl.ds(at, strip), :] = lo
        return carry

    lax.fori_loop(0, levels // strip, dense, 0)

    def rolled(shift):
        return pltpu.roll(bands, lax.rem(shift + 2 * levels, levels), 1)

    wide_r = up(rows, 128)
    diff = lax.broadcasted_iota(jnp.int32, (rows, wide_r), 0) - lax.broadcasted_iota(
        jnp.int32, (rows, wide_r), 1
    )
    near_bands = rolled(-row_start)
    loc = jnp.where(diff == 0, near_bands[0:1, :wide_r], 0.0)
    for o in range(1, edge + 1):
        loc = jnp.where(diff == o, near_bands[o : o + 1, :wide_r], loc)
        loc = jnp.where(diff == -o, pltpu.roll(near_bands, o, 1)[o : o + 1, :wide_r], loc)
    loc_hi, loc_lo = split(loc[:, :rows])
    sub = lax.broadcasted_iota(jnp.int32, (2 * edge, 128), 0)
    lan = lax.broadcasted_iota(jnp.int32, (2 * edge, 128), 1)
    low_bands = rolled(edge - row_start)
    high_bands = rolled(edge - row_start - rows)
    halo_h = jnp.zeros((2 * edge, 128), f32)
    for o in range(edge + 1):
        low = (sub < edge) & (lan < edge) & (edge + sub - lan == o)
        high = (sub >= edge) & (lan >= edge) & (lan < 2 * edge) & (edge + lan - sub == o)
        above = pltpu.roll(high_bands, o, 1) if o else high_bands
        halo_h = jnp.where(low, low_bands[o : o + 1, :128], halo_h)
        halo_h = jnp.where(high, above[o : o + 1, :128], halo_h)
    halo_h = halo_h[:, : 2 * edge]

    def req_wait(i, carry):
        receive(req_ref, req_in, req_send, req_recv, i).wait_recv()
        return carry

    lax.fori_loop(1, tiers, req_wait, 0)
    codes = jnp.transpose(req_in[:, 0, :])
    lane_c = lax.broadcasted_iota(jnp.int32, (cw, sel_c.shape[1]), 1).astype(f32)
    lane_r = lax.broadcasted_iota(jnp.int32, (rw, sel_r.shape[1]), 1).astype(f32)
    for t in range(tiers):
        sel_c[t * cw : (t + 1) * cw, :] = jnp.where(codes[0:cw, t : t + 1] == lane_c, 1.0, 0.0)
        sel_r[t * rw : (t + 1) * rw, :] = jnp.where(
            codes[cw : cw + rw, t : t + 1] == lane_r, 1.0, 0.0
        )
    pick_c = sel_c[...].astype(bf16)
    pick_r = sel_r[...].astype(bf16)
    pack_hi, pack_lo = split(row_pack[...])
    send_r[...] = (mm(pick_r, pack_hi) + mm(pick_r, pack_lo)).reshape(tiers, rw, levels)
    for c in range(2):
        packed = mm_nt(pick_c, col_acc[c].astype(bf16)) + mm_nt(
            pick_c, col_acc[2 + c].astype(bf16)
        )
        send_c[:, :, c * rows : (c + 1) * rows] = packed.reshape(tiers, cw, rows)

    def pack_start(i, carry):
        send(send_r, recv_r, r_send, r_recv, i).start()
        send(send_c, recv_c, c_send, c_recv, i).start()
        return carry

    lax.fori_loop(1, tiers, pack_start, 0)
    recv_c[me] = send_c[me]
    recv_r[me] = send_r[me]

    @pl.when(sy > 0)
    def _():
        for copy in halo(0):
            copy.wait_recv()

    @pl.when(sy < systems - 1)
    def _():
        for copy in halo(1):
            copy.wait_recv()

    def table(ref, count, index):
        value = jnp.zeros((1, wide_q), f32)
        for k in range(count):
            value = jnp.where(index == float(k), ref(k), value)
        return value

    own_count = counts_ref[me].astype(f32)
    near = flag(target < table(lambda k: counts_ref[k].astype(f32), tiers, holder))
    near = near * flag(slot_of < own_count)
    down = kind == 1.0
    w_re = jnp.where(down, level * table(lambda k: coef_ref[0, k], modes, mode), 1.0) * near
    w_im = jnp.where(down, level * table(lambda k: coef_ref[1, k], modes, mode), 0.0) * near
    rate = jnp.where(down, level * table(lambda k: rate_ref[k], modes, mode), 0.0)
    wide_m, wide_b = spread_ref.shape[0], row_at_ref.shape[0]

    def mixing(wide, index, mask, signs):
        from_re, from_im = [], []
        for g in range(slots):
            own = flag((iota((wide, wide_q), 0) == index) & (slot_of == float(g)) & mask)
            for re, im in signs:
                from_re.append(own * re)
                from_im.append(own * im)
        return jnp.concatenate(from_re, axis=0), jnp.concatenate(from_im, axis=0)

    def packets(count, at, mask):
        return flag((iota((count, wide_q), 0) == at) & mask).astype(bf16)

    def place(value, at):
        hi, lo = split(value)
        return mm_nt(hi, at) + mm_nt(lo, at)

    at_c = packets(tiers * cw, holder * float(cw) + rank_c, valid)
    from_re, from_im = mixing(wide_m, mode, valid, ((w_im, -w_re), (w_re, w_im)))
    mix_c = (place(from_re, at_c), place(from_im, at_c))
    from_re, from_im = mixing(wide_b, local_mode, in_block, ((w_im, w_re), (-w_re, w_im)))
    at_row = holder * float(rw) + rank_r
    mix_r = place(from_re, packets(tiers * rw, at_row, in_block)) + place(
        from_im, packets(tiers * rw, at_row + float(rp), in_block)
    )
    site_lane = lax.broadcasted_iota(jnp.int32, (1, levels), 1)
    spread_ref[...] = jnp.zeros_like(spread_ref)
    for k in range(modes):
        spread_ref[k : k + 1, :] = flag(site_lane == site_ref[k])
    row_lane = lax.broadcasted_iota(jnp.int32, (1, rows), 1)
    row_at_ref[...] = jnp.zeros_like(row_at_ref)
    for k in range(block):
        row_at_ref[k : k + 1, :] = flag(row_lane == site_ref[sy * block + k] - row_start)

    def commute(p):
        hi, lo = z_hi[p], z_lo[p]
        g, c = p // 2, p % 2
        neg_hi = h_hi[...]
        both = mm(loc_hi, hi) + mm(hi, neg_hi)
        both += mm(loc_hi, lo) + mm(hi, h_lo[...])
        both += mm(loc_lo, hi) + mm(lo, neg_hi)
        ghost = [halo_st[s, g, c] + (0.5 * step_size) * halo_sl[s, g, c] for s in range(2)]
        extra = mm3(halo_h, jnp.concatenate(ghost, axis=0))
        return both, extra

    for g in range(slots):
        live = flag(own_count > float(g))
        damp = jnp.sum(jnp.where(slot_of == float(g), rate, 0.0), axis=1, keepdims=True) * live
        for c in range(2):
            both, extra = commute(g * 2 + 1 - c)
            p = g * 2 + c
            sign = live if c == 0 else -live
            mid = st[p] + (0.5 * step_size) * sl[p]
            d_buf[p] = sign * both - damp * mid
            d_buf[p, 0:edge, :] += sign * extra[0:edge]
            d_buf[p, rows - edge : rows, :] += sign * extra[edge : 2 * edge]
            base_ref[p] = live * (st[p] + (step_size / 6.0) * sl[p])

    def pack_wait(i, carry):
        receive(send_r, recv_r, r_send, r_recv, i).wait_recv()
        receive(send_c, recv_c, c_send, c_recv, i).wait_recv()
        return carry

    lax.fori_loop(1, tiers, pack_wait, 0)
    got_c = recv_c[...].reshape(tiers * cw, 2 * rows)
    got_r = recv_r[...].reshape(tiers * rw, levels)
    r_ref[...] = mm3(mix_r, got_r)
    c_ref[...] = mm3(mix_c[0], got_c[:, 0:rows]) + mm3(mix_c[1], got_c[:, rows : 2 * rows])

    def finish(i, carry):
        send(req_ref, req_in, req_send, req_recv, i).wait_send()
        send(send_r, recv_r, r_send, r_recv, i).wait_send()
        send(send_c, recv_c, c_send, c_recv, i).wait_send()
        return carry

    lax.fori_loop(1, tiers, finish, 0)

    @pl.when(sy < systems - 1)
    def _():
        for copy in halo(0):
            copy.wait_send()

    @pl.when(sy > 0)
    def _():
        for copy in halo(1):
            copy.wait_send()


def finish_kernel(spread_ref, row_at_ref, c_ref, r_ref, d_ref, base_ref, next_ref, sum_ref):
    p = pl.program_id(0)
    spread = spread_ref[...].astype(bf16)
    row_at = row_at_ref[...]
    wide_m, wide_b = spread_ref.shape[0], row_at_ref.shape[0]
    col = c_ref[pl.ds(pl.multiple_of(p * wide_m, wide_m), wide_m), :]
    col_hi = col.astype(bf16).astype(f32)
    left = jnp.concatenate([col_hi, col - col_hi, row_at, row_at], axis=0)
    row_hi, row_lo = split(r_ref[pl.ds(pl.multiple_of(p * wide_b, wide_b), wide_b), :])
    right = jnp.concatenate([spread, spread, row_hi, row_lo], axis=0)
    slope_next = d_ref[p] + mm(jnp.transpose(left).astype(bf16), right)
    next_ref[0] = slope_next
    sum_ref[0] = base_ref[p] + step_size / 3.0 * slope_next


def shards(tiers, systems, state, slope, counts, links, mode_site, mode_coef, mode_rate, h_bands):
    slots, _, rows, levels = state.shape
    edge = h_bands.shape[0] - 1
    modes = mode_site.shape[0]
    block = modes // systems
    per_slot = links.shape[2]
    total = slots * per_slot
    cp = total // tiers
    rp = 2 * -(-(slots * block) // tiers)
    cw, rw = up(cp, 8), up(2 * rp, 8)
    wide_m, wide_b = up(modes, 16), up(block, 16)
    arrays = (links, counts, mode_site, mode_coef, mode_rate, h_bands, state, slope)
    vmem = pl.BlockSpec(memory_space=pltpu.VMEM)
    hbm = pl.BlockSpec(memory_space=pltpu.HBM)
    planes = slots * 2
    wide_gm = up(slots * modes, 128)
    wide_rp = up(2 * slots * block, 128)
    dma = pltpu.SemaphoreType.DMA
    big = (planes, rows, levels)
    deriv, base, col_mix, row_mix, spread, row_at = pl.pallas_call(
        functools.partial(
            exchange_kernel, (tiers, systems, slots, modes, block, edge, per_slot, rp, cw, rw)
        ),
        out_shape=(
            pltpu.VMEM(big, f32),
            pltpu.VMEM(big, f32),
            pltpu.VMEM((planes * wide_m, rows), f32),
            pltpu.VMEM((planes * wide_b, levels), f32),
            pltpu.VMEM((wide_m, levels), f32),
            pltpu.VMEM((wide_b, rows), f32),
        ),
        in_specs=[hbm] * 8,
        out_specs=(vmem,) * 6,
        scratch_shapes=[
            pltpu.VMEM(links.shape, jnp.int32),
            pltpu.SMEM(counts.shape, jnp.int32),
            pltpu.SMEM(mode_site.shape, jnp.int32),
            pltpu.SMEM(mode_coef.shape, f32),
            pltpu.SMEM(mode_rate.shape, f32),
            pltpu.VMEM(h_bands.shape, f32),
            pltpu.VMEM((planes, rows, levels), f32),
            pltpu.VMEM((planes, rows, levels), f32),
            pltpu.VMEM((planes, rows, levels), bf16),
            pltpu.VMEM((planes, rows, levels), bf16),
            pltpu.VMEM((levels, levels), bf16),
            pltpu.VMEM((levels, levels), bf16),
            pltpu.VMEM((up(edge + 1, 8), levels), f32),
            pltpu.VMEM((tiers, 1, 128), f32),
            pltpu.VMEM((tiers, 1, 128), f32),
            pltpu.VMEM((2, slots, 2, edge, levels), f32),
            pltpu.VMEM((2, slots, 2, edge, levels), f32),
            pltpu.VMEM((4, rows, wide_gm), f32),
            pltpu.VMEM((wide_rp, levels), f32),
            pltpu.VMEM((tiers * cw, wide_gm), f32),
            pltpu.VMEM((tiers * rw, wide_rp), f32),
            pltpu.VMEM((tiers, cw, 2 * rows), f32),
            pltpu.VMEM((tiers, rw, levels), f32),
            pltpu.VMEM((tiers, cw, 2 * rows), f32),
            pltpu.VMEM((tiers, rw, levels), f32),
            dma((2, planes)),
            dma((tiers,)),
            dma((tiers,)),
            dma((2, 2)),
            dma((2, 2)),
            dma((tiers,)),
            dma((tiers,)),
            dma((tiers,)),
            dma((tiers,)),
            dma((6,)),
        ],
        compiler_params=pltpu.CompilerParams(
            collective_id=0, has_side_effects=True, vmem_limit_bytes=32 << 20
        ),
        name="exchange",
    )(*(pltpu.with_memory_space_constraint(x, pltpu.HBM) for x in arrays))
    plane = pl.BlockSpec((1, rows, levels), lambda p: (p, 0, 0))
    outs = pl.pallas_call(
        finish_kernel,
        grid=(planes,),
        out_shape=(jax.ShapeDtypeStruct(big, f32),) * 2,
        in_specs=[vmem] * 6,
        out_specs=(plane, plane),
        compiler_params=pltpu.CompilerParams(vmem_limit_bytes=16 << 20),
        name="finish",
    )(spread, row_at, col_mix, row_mix, deriv, base)
    return tuple(out.reshape(state.shape) for out in outs)


def solution(mesh):
    in_specs = (
        P("tier", None, "sys", None),
        P("tier", None, "sys", None),
        P(),
        P(None, "tier", None),
        P(),
        P(),
        P(),
        P(),
    )
    out_specs = (P("tier", None, "sys", None), P("tier", None, "sys", None))
    body = functools.partial(shards, mesh.shape["tier"], mesh.shape["sys"])
    return jax.shard_map(body, mesh=mesh, in_specs=in_specs, out_specs=out_specs, check_vma=False)
```

```python
import functools

import jax
import jax.numpy as jnp
from jax import lax
from jax.experimental import pallas as pl
from jax.experimental.pallas import tpu as pltpu
from jax.sharding import PartitionSpec as P

step_size = 0.05
MESH = pl.DeviceIdType.MESH
f32 = jnp.float32
bf16 = jnp.bfloat16


def up(value, unit):
    return (value + unit - 1) // unit * unit


def split(value):
    hi = value.astype(bf16)
    lo = (value - hi.astype(f32)).astype(bf16)
    return hi, lo


def mm(a, b):
    return lax.dot_general(a, b, (((1,), (0,)), ((), ())), preferred_element_type=f32)


def mm_nt(a, b):
    return lax.dot_general(a, b, (((1,), (1,)), ((), ())), preferred_element_type=f32)


def mm3(a, b):
    a_hi, a_lo = split(a)
    b_hi, b_lo = split(b)
    return mm(a_hi, b_hi) + (mm(a_hi, b_lo) + mm(a_lo, b_hi))


def banded(diff, bands, edge):
    total = jnp.where(diff == 0, bands[0:1, :], 0.0)
    for o in range(1, edge + 1):
        total = jnp.where(diff == o, bands[o : o + 1, :], total)
        total = jnp.where(diff == -o, pltpu.roll(bands, o, 1)[o : o + 1, :], total)
    return total


def exchange_kernel(
    dims,
    links_hbm,
    counts_hbm,
    site_hbm,
    coef_hbm,
    rate_hbm,
    bands_hbm,
    state_hbm,
    slope_hbm,
    d_buf,
    base_ref,
    c_ref,
    r_ref,
    spread_ref,
    row_at_ref,
    links_ref,
    counts_ref,
    site_ref,
    coef_ref,
    rate_ref,
    bands_ref,
    st,
    sl,
    z_hi,
    z_lo,
    h_hi,
    h_lo,
    bands_pad,
    req_ref,
    req_in,
    halo_st,
    halo_sl,
    col_acc,
    row_pack,
    sel_c,
    sel_r,
    send_c,
    send_r,
    recv_c,
    recv_r,
    load_sem,
    req_send,
    req_recv,
    halo_send,
    halo_recv,
    c_send,
    c_recv,
    r_send,
    r_recv,
    small_sem,
):
    tiers, systems, slots, modes, block, edge, per_slot, rp, cw, rw = dims
    rows, levels = st.shape[1], st.shape[2]
    me = lax.axis_index("tier")
    sy = lax.axis_index("sys")
    planes = slots * 2

    def load(p):
        g, c = p // 2, p % 2
        return (
            pltpu.make_async_copy(state_hbm.at[g, c], st.at[p], load_sem.at[0, p]),
            pltpu.make_async_copy(slope_hbm.at[g, c], sl.at[p], load_sem.at[1, p]),
        )

    small = [
        pltpu.make_async_copy(src, dst, small_sem.at[n])
        for n, (src, dst) in enumerate(
            (
                (links_hbm, links_ref),
                (counts_hbm, counts_ref),
                (site_hbm, site_ref),
                (coef_hbm, coef_ref),
                (rate_hbm, rate_ref),
                (bands_hbm, bands_ref),
            )
        )
    ]
    for copy in small:
        copy.start()
    for p in range(planes):
        for copy in load(p):
            copy.start()

    barrier = pltpu.get_barrier_semaphore()

    def greet(i, carry):
        pl.semaphore_signal(
            barrier, inc=1, device_id=(lax.rem(me + i, tiers), sy), device_id_type=MESH
        )
        return carry

    lax.fori_loop(1, tiers, greet, 0)

    @pl.when(sy > 0)
    def _():
        pl.semaphore_signal(barrier, inc=1, device_id=(me, sy - 1), device_id_type=MESH)

    @pl.when(sy < systems - 1)
    def _():
        pl.semaphore_signal(barrier, inc=1, device_id=(me, sy + 1), device_id_type=MESH)

    total = slots * per_slot
    wide_q = up(total, 128)

    def iota(shape, axis):
        return lax.broadcasted_iota(jnp.int32, shape, axis).astype(f32)

    def flag(where):
        return jnp.where(where, 1.0, 0.0)

    for copy in small:
        copy.wait()
    flat = jnp.zeros((4, wide_q), f32)
    for g in range(slots):
        place = flag(
            iota((per_slot, wide_q), 1) == iota((per_slot, wide_q), 0) + float(g * per_slot)
        )
        flat += mm(links_ref[:, g, :].astype(f32).astype(bf16), place.astype(bf16))
    lane_q = iota((1, wide_q), 1)
    valid = lane_q < float(total)
    mode, kind, level = flat[1:2], flat[2:3], flat[3:4]
    holder = jnp.floor((flat[0:1] + 0.5) * (1.0 / slots))
    target = flat[0:1] - holder * float(slots)
    holder = jnp.where(valid, holder, -1.0)
    slot_of = jnp.where(valid, jnp.floor((lane_q + 0.5) * (1.0 / per_slot)), -1.0)
    first_mode = (sy * block).astype(f32)
    in_block = valid & (mode >= first_mode) & (mode < first_mode + float(block))
    local_mode = mode - first_mode
    has = flag(holder == iota((tiers, wide_q), 0))
    has_r = has * flag(in_block)
    before = flag(iota((wide_q, wide_q), 0) < iota((wide_q, wide_q), 1)).astype(bf16)
    rank_c = jnp.sum(has * mm(has.astype(bf16), before), axis=0, keepdims=True)
    rank_r = jnp.sum(has_r * mm(has_r.astype(bf16), before), axis=0, keepdims=True)
    lane_j = iota((128, wide_q), 0)

    def asked(codes, ranks):
        return mm_nt(codes.astype(bf16), flag(lane_j == ranks).astype(bf16))

    req = asked(has * (target * float(modes) + mode + 1.0), rank_c) - 1.0
    for c in range(2):
        code = (target + float(c * slots)) * float(block) + local_mode + 1.0
        req += asked(has_r * code, rank_r + float(cw + c * rp))
    for t in range(tiers):
        req_ref[t] = req[t : t + 1, :]

    inner = (sy > 0).astype(jnp.int32) + (sy < systems - 1).astype(jnp.int32)
    pl.semaphore_wait(barrier, tiers - 1 + inner)

    def send(src, dst, send_sem, recv_sem, i):
        peer = lax.rem(me + i, tiers)
        return pltpu.make_async_remote_copy(
            src_ref=src.at[peer],
            dst_ref=dst.at[me],
            send_sem=send_sem.at[i],
            recv_sem=recv_sem.at[i],
            device_id=(peer, sy),
            device_id_type=MESH,
        )

    def receive(src, dst, send_sem, recv_sem, i):
        peer = lax.rem(me + tiers - i, tiers)
        return pltpu.make_async_remote_copy(
            src_ref=src.at[peer],
            dst_ref=dst.at[peer],
            send_sem=send_sem.at[i],
            recv_sem=recv_sem.at[i],
            device_id=(peer, sy),
            device_id_type=MESH,
        )

    def req_start(i, carry):
        send(req_ref, req_in, req_send, req_recv, i).start()
        return carry

    lax.fori_loop(1, tiers, req_start, 0)

    def halo(side):
        first = rows - edge if side == 0 else 0
        target = sy + 1 if side == 0 else sy - 1
        return [
            pltpu.make_async_remote_copy(
                src_ref=src.at[:, :, pl.ds(first, edge), :],
                dst_ref=dst.at[side],
                send_sem=halo_send.at[side, n],
                recv_sem=halo_recv.at[side, n],
                device_id=(me, target),
                device_id_type=MESH,
            )
            for n, (src, dst) in enumerate(((state_hbm, halo_st), (slope_hbm, halo_sl)))
        ]

    @pl.when(sy < systems - 1)
    def _():
        for copy in halo(0):
            copy.start()

    @pl.when(sy > 0)
    def _():
        for copy in halo(1):
            copy.start()

    @pl.when(sy == 0)
    def _():
        halo_st[0] = jnp.zeros_like(halo_st[0])
        halo_sl[0] = jnp.zeros_like(halo_sl[0])

    @pl.when(sy == systems - 1)
    def _():
        halo_st[1] = jnp.zeros_like(halo_st[1])
        halo_sl[1] = jnp.zeros_like(halo_sl[1])

    req_in[me] = req_ref[me]
    row_pack[...] = jnp.zeros_like(row_pack)
    width = col_acc.shape[-1]
    lane_gm = iota((1, width), 1)
    lane_slot = jnp.floor((lane_gm + 0.5) * (1.0 / modes))
    lane_mode = lane_gm - lane_slot * float(modes)
    lane_site = jnp.zeros((1, width), jnp.int32)
    for k in range(modes):
        lane_site = jnp.where(lane_mode == float(k), site_ref[k], lane_site)
    level_at = lax.broadcasted_iota(jnp.int32, (levels, width), 0)
    for g in range(slots):
        pick = jnp.where((level_at == lane_site) & (lane_slot == float(g)), 1.0, 0.0).astype(bf16)
        for c in range(2):
            p = g * 2 + c
            for copy in load(p):
                copy.wait()
            hi, lo = split(st[p] + (0.5 * step_size) * sl[p])
            z_hi[p] = hi
            z_lo[p] = lo
            col_hi = mm(hi, pick)
            col_lo = mm(lo, pick)
            if g == 0:
                col_acc[c] = col_hi
                col_acc[2 + c] = col_lo
            else:
                col_acc[c] += col_hi
                col_acc[2 + c] += col_lo
    for c in range(2):
        for g in range(slots):
            for k in range(block):
                at = jnp.clip(site_ref[sy * block + k] - sy * rows, 0, rows - 1)
                p = g * 2 + c
                row = st[p, pl.ds(at, 1), :] + (0.5 * step_size) * sl[p, pl.ds(at, 1), :]
                dest = (c * slots + g) * block + k
                row_pack[dest : dest + 1, :] = row

    def req_wait(i, carry):
        receive(req_ref, req_in, req_send, req_recv, i).wait_recv()
        return carry

    lax.fori_loop(1, tiers, req_wait, 0)
    codes = jnp.transpose(req_in[:, 0, :])
    lane_c = lax.broadcasted_iota(jnp.int32, (cw, sel_c.shape[1]), 1).astype(f32)
    lane_r = lax.broadcasted_iota(jnp.int32, (rw, sel_r.shape[1]), 1).astype(f32)
    for t in range(tiers):
        sel_c[t * cw : (t + 1) * cw, :] = jnp.where(codes[0:cw, t : t + 1] == lane_c, 1.0, 0.0)
        sel_r[t * rw : (t + 1) * rw, :] = jnp.where(
            codes[cw : cw + rw, t : t + 1] == lane_r, 1.0, 0.0
        )
    pick_c = sel_c[...].astype(bf16)
    pick_r = sel_r[...].astype(bf16)
    pack_hi, pack_lo = split(row_pack[...])
    send_r[...] = (mm(pick_r, pack_hi) + mm(pick_r, pack_lo)).reshape(tiers, rw, levels)
    for c in range(2):
        packed = mm_nt(pick_c, col_acc[c].astype(bf16)) + mm_nt(
            pick_c, col_acc[2 + c].astype(bf16)
        )
        send_c[:, :, c * rows : (c + 1) * rows] = packed.reshape(tiers, cw, rows)

    def pack_start(i, carry):
        send(send_r, recv_r, r_send, r_recv, i).start()
        send(send_c, recv_c, c_send, c_recv, i).start()
        return carry

    lax.fori_loop(1, tiers, pack_start, 0)
    recv_c[me] = send_c[me]
    recv_r[me] = send_r[me]

    row_start = sy * rows
    bands_pad[...] = jnp.zeros_like(bands_pad)
    bands_pad[0 : edge + 1, :] = bands_ref[...]
    bands = bands_pad[...]
    strip = min(128, levels)

    def dense(i, carry):
        at = pl.multiple_of(i * strip, strip)
        diff = (
            lax.broadcasted_iota(jnp.int32, (strip, levels), 0)
            + at
            - lax.broadcasted_iota(jnp.int32, (strip, levels), 1)
        )
        hi, lo = split(-banded(diff, bands, edge))
        h_hi[pl.ds(at, strip), :] = hi
        h_lo[pl.ds(at, strip), :] = lo
        return carry

    lax.fori_loop(0, levels // strip, dense, 0)

    def rolled(shift):
        return pltpu.roll(bands, lax.rem(shift + 2 * levels, levels), 1)

    wide_r = up(rows, 128)
    diff = lax.broadcasted_iota(jnp.int32, (rows, wide_r), 0) - lax.broadcasted_iota(
        jnp.int32, (rows, wide_r), 1
    )
    near_bands = rolled(-row_start)
    loc = jnp.where(diff == 0, near_bands[0:1, :wide_r], 0.0)
    for o in range(1, edge + 1):
        loc = jnp.where(diff == o, near_bands[o : o + 1, :wide_r], loc)
        loc = jnp.where(diff == -o, pltpu.roll(near_bands, o, 1)[o : o + 1, :wide_r], loc)
    loc_hi, loc_lo = split(loc[:, :rows])
    sub = lax.broadcasted_iota(jnp.int32, (2 * edge, 128), 0)
    lan = lax.broadcasted_iota(jnp.int32, (2 * edge, 128), 1)
    low_bands = rolled(edge - row_start)
    high_bands = rolled(edge - row_start - rows)
    halo_h = jnp.zeros((2 * edge, 128), f32)
    for o in range(edge + 1):
        low = (sub < edge) & (lan < edge) & (edge + sub - lan == o)
        high = (sub >= edge) & (lan >= edge) & (lan < 2 * edge) & (edge + lan - sub == o)
        above = pltpu.roll(high_bands, o, 1) if o else high_bands
        halo_h = jnp.where(low, low_bands[o : o + 1, :128], halo_h)
        halo_h = jnp.where(high, above[o : o + 1, :128], halo_h)
    halo_h = halo_h[:, : 2 * edge]

    @pl.when(sy > 0)
    def _():
        for copy in halo(0):
            copy.wait_recv()

    @pl.when(sy < systems - 1)
    def _():
        for copy in halo(1):
            copy.wait_recv()

    def table(ref, count, index):
        value = jnp.zeros((1, wide_q), f32)
        for k in range(count):
            value = jnp.where(index == float(k), ref(k), value)
        return value

    own_count = counts_ref[me].astype(f32)
    near = flag(target < table(lambda k: counts_ref[k].astype(f32), tiers, holder))
    near = near * flag(slot_of < own_count)
    down = kind == 1.0
    w_re = jnp.where(down, level * table(lambda k: coef_ref[0, k], modes, mode), 1.0) * near
    w_im = jnp.where(down, level * table(lambda k: coef_ref[1, k], modes, mode), 0.0) * near
    rate = jnp.where(down, level * table(lambda k: rate_ref[k], modes, mode), 0.0)
    wide_m, wide_b = spread_ref.shape[0], row_at_ref.shape[0]

    def mixing(wide, index, mask, signs):
        from_re, from_im = [], []
        for g in range(slots):
            own = flag((iota((wide, wide_q), 0) == index) & (slot_of == float(g)) & mask)
            for re, im in signs:
                from_re.append(own * re)
                from_im.append(own * im)
        return jnp.concatenate(from_re, axis=0), jnp.concatenate(from_im, axis=0)

    def packets(count, at, mask):
        return flag((iota((count, wide_q), 0) == at) & mask).astype(bf16)

    def place(value, at):
        hi, lo = split(value)
        return mm_nt(hi, at) + mm_nt(lo, at)

    at_c = packets(tiers * cw, holder * float(cw) + rank_c, valid)
    from_re, from_im = mixing(wide_m, mode, valid, ((w_im, -w_re), (w_re, w_im)))
    mix_c = (place(from_re, at_c), place(from_im, at_c))
    from_re, from_im = mixing(wide_b, local_mode, in_block, ((w_im, w_re), (-w_re, w_im)))
    at_row = holder * float(rw) + rank_r
    mix_r = place(from_re, packets(tiers * rw, at_row, in_block)) + place(
        from_im, packets(tiers * rw, at_row + float(rp), in_block)
    )
    site_lane = lax.broadcasted_iota(jnp.int32, (1, levels), 1)
    spread_ref[...] = jnp.zeros_like(spread_ref)
    for k in range(modes):
        spread_ref[k : k + 1, :] = flag(site_lane == site_ref[k])
    row_lane = lax.broadcasted_iota(jnp.int32, (1, rows), 1)
    row_at_ref[...] = jnp.zeros_like(row_at_ref)
    for k in range(block):
        row_at_ref[k : k + 1, :] = flag(row_lane == site_ref[sy * block + k] - row_start)

    def commute(p):
        hi, lo = z_hi[p], z_lo[p]
        g, c = p // 2, p % 2
        neg_hi = h_hi[...]
        both = mm(loc_hi, hi) + mm(hi, neg_hi)
        both += mm(loc_hi, lo) + mm(hi, h_lo[...])
        both += mm(loc_lo, hi) + mm(lo, neg_hi)
        ghost = [halo_st[s, g, c] + (0.5 * step_size) * halo_sl[s, g, c] for s in range(2)]
        extra = mm3(halo_h, jnp.concatenate(ghost, axis=0))
        return both, extra

    for g in range(slots):
        live = flag(own_count > float(g))
        damp = jnp.sum(jnp.where(slot_of == float(g), rate, 0.0), axis=1, keepdims=True) * live
        for c in range(2):
            both, extra = commute(g * 2 + 1 - c)
            p = g * 2 + c
            sign = live if c == 0 else -live
            mid = st[p] + (0.5 * step_size) * sl[p]
            d_buf[p] = sign * both - damp * mid
            d_buf[p, 0:edge, :] += sign * extra[0:edge]
            d_buf[p, rows - edge : rows, :] += sign * extra[edge : 2 * edge]
            base_ref[p] = live * (st[p] + (step_size / 6.0) * sl[p])

    def pack_wait(i, carry):
        receive(send_r, recv_r, r_send, r_recv, i).wait_recv()
        receive(send_c, recv_c, c_send, c_recv, i).wait_recv()
        return carry

    lax.fori_loop(1, tiers, pack_wait, 0)
    got_c = recv_c[...].reshape(tiers * cw, 2 * rows)
    got_r = recv_r[...].reshape(tiers * rw, levels)
    r_ref[...] = mm3(mix_r, got_r)
    c_ref[...] = mm3(mix_c[0], got_c[:, 0:rows]) + mm3(mix_c[1], got_c[:, rows : 2 * rows])

    def finish(i, carry):
        send(req_ref, req_in, req_send, req_recv, i).wait_send()
        send(send_r, recv_r, r_send, r_recv, i).wait_send()
        send(send_c, recv_c, c_send, c_recv, i).wait_send()
        return carry

    lax.fori_loop(1, tiers, finish, 0)

    @pl.when(sy < systems - 1)
    def _():
        for copy in halo(0):
            copy.wait_send()

    @pl.when(sy > 0)
    def _():
        for copy in halo(1):
            copy.wait_send()


def finish_kernel(spread_ref, row_at_ref, c_ref, r_ref, d_ref, base_ref, next_ref, sum_ref):
    p = pl.program_id(0)
    spread = spread_ref[...].astype(bf16)
    row_at = row_at_ref[...]
    wide_m, wide_b = spread_ref.shape[0], row_at_ref.shape[0]
    col = c_ref[pl.ds(pl.multiple_of(p * wide_m, wide_m), wide_m), :]
    col_hi = col.astype(bf16).astype(f32)
    left = jnp.concatenate([col_hi, col - col_hi, row_at, row_at], axis=0)
    row_hi, row_lo = split(r_ref[pl.ds(pl.multiple_of(p * wide_b, wide_b), wide_b), :])
    right = jnp.concatenate([spread, spread, row_hi, row_lo], axis=0)
    slope_next = d_ref[p] + mm(jnp.transpose(left).astype(bf16), right)
    next_ref[0] = slope_next
    sum_ref[0] = base_ref[p] + step_size / 3.0 * slope_next


def shards(tiers, systems, state, slope, counts, links, mode_site, mode_coef, mode_rate, h_bands):
    slots, _, rows, levels = state.shape
    edge = h_bands.shape[0] - 1
    modes = mode_site.shape[0]
    block = modes // systems
    per_slot = links.shape[2]
    total = slots * per_slot
    cp = total // tiers
    rp = 2 * -(-(slots * block) // tiers)
    cw, rw = up(cp, 8), up(2 * rp, 8)
    wide_m, wide_b = up(modes, 16), up(block, 16)
    arrays = (links, counts, mode_site, mode_coef, mode_rate, h_bands, state, slope)
    vmem = pl.BlockSpec(memory_space=pltpu.VMEM)
    hbm = pl.BlockSpec(memory_space=pltpu.HBM)
    planes = slots * 2
    wide_gm = up(slots * modes, 128)
    wide_rp = up(2 * slots * block, 128)
    dma = pltpu.SemaphoreType.DMA
    big = (planes, rows, levels)
    deriv, base, col_mix, row_mix, spread, row_at = pl.pallas_call(
        functools.partial(
            exchange_kernel, (tiers, systems, slots, modes, block, edge, per_slot, rp, cw, rw)
        ),
        out_shape=(
            pltpu.VMEM(big, f32),
            pltpu.VMEM(big, f32),
            pltpu.VMEM((planes * wide_m, rows), f32),
            pltpu.VMEM((planes * wide_b, levels), f32),
            pltpu.VMEM((wide_m, levels), f32),
            pltpu.VMEM((wide_b, rows), f32),
        ),
        in_specs=[hbm] * 8,
        out_specs=(vmem,) * 6,
        scratch_shapes=[
            pltpu.VMEM(links.shape, jnp.int32),
            pltpu.SMEM(counts.shape, jnp.int32),
            pltpu.SMEM(mode_site.shape, jnp.int32),
            pltpu.SMEM(mode_coef.shape, f32),
            pltpu.SMEM(mode_rate.shape, f32),
            pltpu.VMEM(h_bands.shape, f32),
            pltpu.VMEM((planes, rows, levels), f32),
            pltpu.VMEM((planes, rows, levels), f32),
            pltpu.VMEM((planes, rows, levels), bf16),
            pltpu.VMEM((planes, rows, levels), bf16),
            pltpu.VMEM((levels, levels), bf16),
            pltpu.VMEM((levels, levels), bf16),
            pltpu.VMEM((up(edge + 1, 8), levels), f32),
            pltpu.VMEM((tiers, 1, 128), f32),
            pltpu.VMEM((tiers, 1, 128), f32),
            pltpu.VMEM((2, slots, 2, edge, levels), f32),
            pltpu.VMEM((2, slots, 2, edge, levels), f32),
            pltpu.VMEM((4, rows, wide_gm), f32),
            pltpu.VMEM((wide_rp, levels), f32),
            pltpu.VMEM((tiers * cw, wide_gm), f32),
            pltpu.VMEM((tiers * rw, wide_rp), f32),
            pltpu.VMEM((tiers, cw, 2 * rows), f32),
            pltpu.VMEM((tiers, rw, levels), f32),
            pltpu.VMEM((tiers, cw, 2 * rows), f32),
            pltpu.VMEM((tiers, rw, levels), f32),
            dma((2, planes)),
            dma((tiers,)),
            dma((tiers,)),
            dma((2, 2)),
            dma((2, 2)),
            dma((tiers,)),
            dma((tiers,)),
            dma((tiers,)),
            dma((tiers,)),
            dma((6,)),
        ],
        compiler_params=pltpu.CompilerParams(
            collective_id=0, has_side_effects=True, vmem_limit_bytes=32 << 20
        ),
        name="exchange",
    )(*(pltpu.with_memory_space_constraint(x, pltpu.HBM) for x in arrays))
    plane = pl.BlockSpec((1, rows, levels), lambda p: (p, 0, 0))
    outs = pl.pallas_call(
        finish_kernel,
        grid=(planes,),
        out_shape=(jax.ShapeDtypeStruct(big, f32),) * 2,
        in_specs=[vmem] * 6,
        out_specs=(plane, plane),
        compiler_params=pltpu.CompilerParams(vmem_limit_bytes=16 << 20),
        name="finish",
    )(spread, row_at, col_mix, row_mix, deriv, base)
    return tuple(out.reshape(state.shape) for out in outs)


def solution(mesh):
    in_specs = (
        P("tier", None, "sys", None),
        P("tier", None, "sys", None),
        P(),
        P(None, "tier", None),
        P(),
        P(),
        P(),
        P(),
    )
    out_specs = (P("tier", None, "sys", None), P("tier", None, "sys", None))
    body = functools.partial(shards, mesh.shape["tier"], mesh.shape["sys"])
    return jax.shard_map(body, mesh=mesh, in_specs=in_specs, out_specs=out_specs, check_vma=False)
```
